32 devices in a mesh: fsdp: 8 (over y, x, core), ctx: 2 (over z_hi), tp: 2 (over z_lo).
Axes of the slice: x: 2, y: 2, z: 4 (z_hi: 2, z_lo: 2; z = z_hi * 2 + z_lo), core: 2. Of those that a mesh axis runs over, the one named last changes fastest.
Arguments:
- layer_in: bfloat16 [16, 1024, 1024], P('fsdp', 'ctx'), may hold values from -6 to 6
- lengths: int32 [16], P('fsdp'), may hold values from 256 to 1024, as said below
- out_grad: bfloat16 [16, 1024, 1024], P('fsdp', 'ctx'), may hold values from -6 to 6
- query_weight: bfloat16 [1024, 1024], P('fsdp', 'tp'), may hold values from -0.1875 to 0.1875
- key_weight: bfloat16 [1024, 1024], P('fsdp', 'tp'), may hold values from -0.1875 to 0.1875
- value_weight: bfloat16 [1024, 1024], P('fsdp', 'tp'), may hold values from -0.1875 to 0.1875
- out_weight: bfloat16 [1024, 1024], P('tp', 'fsdp'), may hold values from -3 to 3
- up_weight: bfloat16 [1024, 4096], P('fsdp', 'tp'), may hold values from -0.1875 to 0.1875
- down_weight: bfloat16 [4096, 1024], P('tp', 'fsdp'), may hold values from -0.09375 to 0.09375
- query_bias: float32 [1024], P('tp'), may hold values from -4 to 4
- value_bias: float32 [1024], P('tp'), may hold values from -4 to 4
- out_bias: float32 [1024], replicated, may hold values from -4 to 4
- up_bias: float32 [4096], P('tp'), may hold values from -4 to 4
- down_bias: float32 [1024], replicated, may hold values from -4 to 4
- norm_gain: float32 [1024], replicated, may hold values from 0.5 to 1.5
- norm_bias: float32 [1024], replicated, may hold values from -0.5 to 0.5
- final_gain: float32 [1024], replicated, may hold values from 0.5 to 1.5
- final_bias: float32 [1024], replicated, may hold values from -0.5 to 0.5
Outputs:
- layer_out: bfloat16 [16, 1024, 1024], P('fsdp', 'ctx')
- input_grad: float32 [16, 1024, 1024], P('fsdp', 'ctx')
- query_weight_grad: float32 [1024, 1024], P('fsdp', 'tp')
- key_weight_grad: float32 [1024, 1024], P('fsdp', 'tp')
- value_weight_grad: float32 [1024, 1024], P('fsdp', 'tp')
- out_weight_grad: float32 [1024, 1024], P('tp', 'fsdp')
- up_weight_grad: float32 [1024, 4096], P('fsdp', 'tp')
- down_weight_grad: float32 [4096, 1024], P('tp', 'fsdp')
- query_bias_grad: float32 [1024], P('tp')
- value_bias_grad: float32 [1024], P('tp')
- out_bias_grad: float32 [1024], replicated
- up_bias_grad: float32 [4096], P('tp')
- down_bias_grad: float32 [1024], replicated
- norm_gain_grad: float32 [1024], replicated
- norm_bias_grad: float32 [1024], replicated
- final_gain_grad: float32 [1024], replicated
- final_bias_grad: float32 [1024], replicated
The draws below stay inside these ranges and needn't reach their ends.
Inputs may be any that keep to these rules, and one draw needn't show every extreme that they name: Sequence lengths; some sequence has exactly 256 and some exactly 1024.
All inputs are finite; a program needn't handle non-finite values.
Results may differ from the reference program's by a relative error of at most 0.03.
Values may be sent and summed in bfloat16 or wider, within the bound.
No kernel may reach another device: no remote copies, remote signals or barrier semaphores. Data moves between devices by JAX's collectives and lax.ppermute only.
A program may use at most 256 MiB of HBM per device.

```python
import jax
import jax.numpy as jnp
from jax import lax

D = 1024
H = 16
DH = 64
FF = 4096
SLOT = 1024
SEQS = 16


def draw_lengths(key, part):
    drawn = jax.random.randint(jax.random.fold_in(key, 11), (SEQS,), SLOT // 4, SLOT + 1)
    order = jax.random.permutation(jax.random.fold_in(key, 12), SEQS)
    drawn = drawn.at[order[0]].set(SLOT)
    drawn = drawn.at[order[1]].set(SLOT // 4)
    return drawn.astype(jnp.int32)


def block_levels(stream_key, extent, split, low, top_value):
    def one(dim, shards_of):
        draws = jax.random.uniform(jax.random.fold_in(jax.random.fold_in(stream_key, 6), dim), (shards_of,), jnp.float32, low / len(split), top_value / len(split))
        return jnp.repeat(jnp.exp(draws), extent[dim] // shards_of).reshape((-1,) + (1,) * (len(extent) - dim - 1))

    factor_of = one(*split[0])
    for cut in split[1:]:
        factor_of = factor_of * one(*cut)
    return factor_of


def bell_draw(stream_key, dims, width, reach, split=(), kind=jnp.bfloat16):
    values = width * jax.random.normal(stream_key, dims, jnp.float32)
    if split:
        values = values * block_levels(stream_key, dims, split, -0.22, 0.18)
    return jnp.clip(values, -reach, reach).astype(kind)


def setup_inputs(seed: int = 0) -> dict:
    seeds = jax.random.split(jax.random.key(seed), 19)
    return {
        "layer_in": bell_draw(seeds[0], (SEQS, SLOT, D), 1.0, 6.0, ((0, 8), (1, 2))),
        "lengths": draw_lengths(jax.random.fold_in(seeds[18], 71), 0),
        "out_grad": bell_draw(seeds[2], (SEQS, SLOT, D), 1.0, 6.0, ((0, 8), (1, 2))),
        "query_weight": bell_draw(seeds[3], (D, D), D ** -0.5, 0.1875, ((0, 8), (1, 2))),
        "key_weight": bell_draw(seeds[4], (D, D), D ** -0.5, 0.1875, ((0, 8), (1, 2))),
        "value_weight": bell_draw(seeds[5], (D, D), D ** -0.5, 0.1875, ((0, 8), (1, 2))),
        "out_weight": bell_draw(seeds[6], (D, D), 4 ** -0.5, 3.0, ((0, 2), (1, 8))),
        "up_weight": bell_draw(seeds[7], (D, FF), D ** -0.5, 0.1875, ((0, 8), (1, 2))),
        "down_weight": bell_draw(seeds[8], (FF, D), FF ** -0.5, 0.09375, ((0, 2), (1, 8))),
        "query_bias": bell_draw(seeds[9], (D,), 1.0, 4.0, ((0, 2),), jnp.float32),
        "value_bias": bell_draw(seeds[10], (D,), 0.3, 4.0, ((0, 2),), jnp.float32),
        "out_bias": bell_draw(seeds[11], (D,), 0.5, 4.0, (), jnp.float32),
        "up_bias": bell_draw(seeds[12], (FF,), 0.5, 4.0, ((0, 2),), jnp.float32),
        "down_bias": bell_draw(seeds[13], (D,), 0.5, 4.0, (), jnp.float32),
        "norm_gain": jnp.clip(1.0 + 0.1 * jax.random.normal(seeds[14], (D,), jnp.float32), 0.5, 1.5),
        "norm_bias": jnp.clip(jax.random.uniform(seeds[15], (D,), jnp.float32, -0.5, 0.5), -0.5, 0.5),
        "final_gain": jnp.clip(1.0 + 0.1 * jax.random.normal(seeds[16], (D,), jnp.float32), 0.5, 1.5),
        "final_bias": jnp.clip(jax.random.uniform(seeds[17], (D,), jnp.float32, -0.5, 0.5), -0.5, 0.5),
    }


@jax.custom_vjp
def low(v):
    return lax.optimization_barrier(v.astype(jnp.bfloat16)).astype(jnp.float32)

@jax.custom_vjp
def low_back(v):
    return v

def low_keep(v):
    return (low(v), None)

def low_pass(kept, grad):
    return (grad,)

def back_keep(v):
    return (v, None)

def back_low(kept, grad):
    return (low(grad),)
low.defvjp(low_keep, low_pass)
low_back.defvjp(back_keep, back_low)
norm_eps = 1e-05
masked_score = -1e+30

def rounded_both(value):
    return low(low_back(value))

def fine(left, right):
    return jnp.dot(left, right, precision=lax.Precision.HIGHEST, preferred_element_type=jnp.float32)

def layer_norm(hidden, gain, offset):
    centred = hidden - lax.optimization_barrier(jnp.mean(hidden, axis=-1, keepdims=True))
    spread = lax.optimization_barrier(jnp.mean(centred * centred, axis=-1, keepdims=True))
    return centred * lax.rsqrt(spread + norm_eps) * gain + offset

def layer(stream, lengths, query_weight, key_weight, value_weight, out_weight, up_weight, down_weight, query_bias, value_bias, out_bias, up_bias, down_bias, norm_gain, norm_bias, final_gain, final_bias):
    scale = DH ** (-0.5)

    def one_sequence(carry, item):
        rows, length = item
        queries = rounded_both((fine(rows, query_weight) + query_bias) * scale).reshape(SLOT, H, DH)
        keys = rounded_both(fine(rows, key_weight)).reshape(SLOT, H, DH)
        values = rounded_both(fine(rows, value_weight) + value_bias).reshape(SLOT, H, DH)
        scores = low_back(jnp.einsum('qhd,khd->hqk', queries, keys, precision=lax.Precision.HIGHEST))
        valid = lax.iota(jnp.int32, SLOT) < length
        scores = jnp.where(valid[None, None, :], scores, masked_score)
        prob = low(jax.nn.softmax(scores, axis=-1))
        merged = jnp.einsum('hqk,khd->qhd', prob, values, precision=lax.Precision.HIGHEST)
        merged = rounded_both(merged.reshape(SLOT, D))
        attn = low_back(fine(merged, out_weight) + out_bias)
        normed = layer_norm(rows + attn, norm_gain, norm_bias)
        upper = low_back(fine(low(normed), up_weight) + up_bias)
        activated = low(jax.nn.gelu(upper, approximate=False))
        ffn = low_back(fine(activated, down_weight) + down_bias)
        return (carry, layer_norm(normed + ffn, final_gain, final_bias))
    _, outputs = lax.scan(jax.checkpoint(one_sequence), jnp.float32(0.0), (stream, lengths))
    return outputs

def reference(layer_in, lengths, out_grad, query_weight, key_weight, value_weight, out_weight, up_weight, down_weight, query_bias, value_bias, out_bias, up_bias, down_bias, norm_gain, norm_bias, final_gain, final_bias):
    inputs = (layer_in, query_weight, key_weight, value_weight, out_weight, up_weight, down_weight, query_bias, value_bias, out_bias, up_bias, down_bias, norm_gain, norm_bias, final_gain, final_bias)
    floats = [item.astype(jnp.float32) for item in inputs]

    def closed(*values):
        return layer(values[0], lengths, *values[1:])
    result, backward = jax.vjp(closed, *floats)
    valid = (lax.iota(jnp.int32, SLOT)[None, :] < lengths[:, None]).astype(jnp.float32)
    grads = backward(out_grad.astype(jnp.float32) * valid[:, :, None])
    return (result.astype(jnp.bfloat16), grads[0], grads[1], grads[2], grads[3], grads[4], grads[5], grads[6], grads[7], grads[8], grads[9], grads[10], grads[11], grads[12], grads[13], grads[14], grads[15])
```

```python
import functools

import jax
import jax.numpy as jnp
from jax import lax
from jax.experimental import pallas as pl
from jax.experimental.pallas import tpu as pltpu
from jax.sharding import PartitionSpec as P

DH = 64
PAIR = 2 * DH
ROWS = 256

norm_eps = 1e-05
masked_score = -1e30
BF16 = jnp.bfloat16
F32 = jnp.float32
AXES = ("fsdp", "ctx", "tp")


def send(value, target):
    fsdp, ctx, tp = (lax.axis_size(axis) for axis in AXES)
    pairs = []
    for f in range(fsdp):
        for h in range(ctx):
            for t in range(tp):
                plane, core, high, low = target(f // 2, f % 2, h, t)
                pairs.append(((f * ctx + h) * tp + t, ((2 * plane + core) * ctx + high) * tp + low))
    return lax.ppermute(value, AXES, pairs)


def to_core(value):
    return send(value, lambda p, c, h, t: (p, 1 - c, h, t))


def to_x(value):
    return send(value, lambda p, c, h, t: (p ^ 1, c, h, t))


def to_y(value):
    return send(value, lambda p, c, h, t: (p ^ 2, c, h, t))


def to_high(value):
    return send(value, lambda p, c, h, t: (p, c, 1 - h, t))


def to_low(value):
    return send(value, lambda p, c, h, t: (p, c, h, 1 - t))


def to_turned(value):
    return send(value, lambda p, c, h, t: (p, h, c, t))


def to_first(value):
    return send(value, lambda p, c, h, t: (p, t, h, c))


def to_second(value):
    return send(value, lambda p, c, h, t: (p, t, h, 1 - c))


def from_second(value):
    return send(value, lambda p, c, h, t: (p, 1 - t, h, c))


def plane_groups():
    fsdp = lax.axis_size("fsdp")
    return [[2 * p + c for p in range(fsdp // 2)] for c in range(2)]


def gather_rows(shard):
    first = to_first(shard)
    second = to_second(shard)
    unit = jnp.concatenate([first, second], axis=0)
    planes = lax.axis_size("fsdp") // 2
    if planes != 4:
        return lax.all_gather(unit, "fsdp", axis=0, tiled=True, axis_index_groups=plane_groups())
    half = shard.shape[0]
    over_x = to_x(unit)
    over_y = to_y(unit)
    far_first = to_y(over_x[:half])
    far_second = to_x(over_y[half:])
    return jnp.concatenate([unit, over_x, over_y, far_first, far_second], axis=0)


def scatter_rows(rows_of, half):
    planes = lax.axis_size("fsdp") // 2
    if planes != 4:
        whole = rows_of(0, 2 * planes * half)
        mine = lax.psum_scatter(
            whole, "fsdp", scatter_dimension=0, tiled=True, axis_index_groups=plane_groups()
        )
    else:
        far_first = to_y(rows_of(6 * half, 7 * half))
        far_second = to_x(rows_of(7 * half, 8 * half))
        over_x = rows_of(2 * half, 4 * half)
        over_y = rows_of(4 * half, 6 * half)
        over_x = jnp.concatenate([added(over_x[:half], far_first), over_x[half:]], axis=0)
        over_y = jnp.concatenate([over_y[:half], added(over_y[half:], far_second)], axis=0)
        over_x = to_x(over_x)
        over_y = to_y(over_y)
        mine = rows_of(0, 2 * half).astype(F32) + over_x.astype(F32) + over_y.astype(F32)
        mine = mine.astype(BF16)
    first = to_first(mine[:half])
    second = from_second(mine[half:])
    return added(first, second)


def added(one, other):
    return (one.astype(F32) + other.astype(F32)).astype(BF16)


def summed_high(part):
    return part.astype(F32) + to_high(part).astype(F32)


def summed_all(vector):
    fsdp = lax.axis_size("fsdp")
    if fsdp != 8:
        return lax.psum(vector, AXES)
    for step in (to_core, to_x, to_y, to_low, to_high):
        vector = vector + step(vector)
    return vector


def turned_columns(value, key, width):
    lead = value.shape[:-1]
    blocks = value.shape[-1] // width
    value = value.reshape(lead + (blocks, width))
    bit = 1
    while bit < blocks:
        swapped = value.reshape(lead + (blocks // (2 * bit), 2, bit, width))
        swapped = swapped[..., ::-1, :, :].reshape(value.shape)
        value = jnp.where((key & bit) != 0, swapped, value)
        bit *= 2
    return value.reshape(lead + (blocks * width,))


def product(left, right, out=F32):
    return jnp.dot(left, right, preferred_element_type=F32).astype(out)


def product_back(left, right, out=F32):
    return lax.dot_general(
        left, right, (((1,), (1,)), ((), ())), preferred_element_type=F32
    ).astype(out)


def row_product(left, right, out=BF16):
    return lax.dot_general(
        left, right, (((0,), (0,)), ((), ())), preferred_element_type=F32
    ).astype(out)


def attend_kernel(qkv_ref, bias_ref, out_ref, log_ref):
    rows = qkv_ref.shape[0]
    low = lax.broadcasted_iota(jnp.int32, (1, PAIR), 1) < DH
    keys = qkv_ref[:, PAIR : 2 * PAIR]
    values = qkv_ref[:, 2 * PAIR :]
    bias = bias_ref[...]
    zero = jnp.zeros((), BF16)
    picks = (low, jnp.logical_not(low))
    head_values = [jnp.where(pick, values, zero) for pick in picks]
    for tile in range(rows // ROWS):
        at = slice(tile * ROWS, (tile + 1) * ROWS)
        query = qkv_ref[at, :PAIR]
        out = jnp.zeros((ROWS, PAIR), F32)
        logs = jnp.zeros((ROWS, PAIR), F32)
        for head in range(2):
            mine = jnp.where(picks[head], query, zero)
            scores = product_back(mine, keys) + bias
            top = jnp.max(scores, axis=1, keepdims=True)
            weights = jnp.exp(scores - top)
            total = jnp.sum(weights, axis=1, keepdims=True)
            out = out + product(weights.astype(BF16), head_values[head]) / total
            logs = jnp.where(picks[head], top + jnp.log(total), logs)
        out_ref[at, :] = out.astype(BF16)
        log_ref[at, :] = logs


def attend(qkv, bias):
    rows = qkv.shape[0]
    pairs = qkv.shape[1] // (3 * PAIR)
    flops = 2 * 2 * 2 * pairs * rows * rows * DH
    return pl.pallas_call(
        attend_kernel,
        grid=(pairs,),
        in_specs=[
            pl.BlockSpec((rows, 3 * PAIR), lambda i: (0, i)),
            pl.BlockSpec((1, rows), lambda i: (0, 0)),
        ],
        out_specs=[
            pl.BlockSpec((rows, PAIR), lambda i: (0, i)),
            pl.BlockSpec((rows, PAIR), lambda i: (0, i)),
        ],
        out_shape=[
            jax.ShapeDtypeStruct((rows, pairs * PAIR), BF16),
            jax.ShapeDtypeStruct((rows, pairs * PAIR), F32),
        ],
        cost_estimate=pl.CostEstimate(
            flops=4 * flops, bytes_accessed=8 * rows * pairs * PAIR * 2,
            transcendentals=2 * pairs * rows * rows,
        ),
        name="attend",
    )(qkv, bias)


def attend_back_kernel(qkv_ref, bias_ref, out_ref, log_ref, grad_ref, result_ref, key_acc, value_acc):
    rows = qkv_ref.shape[0]
    low = lax.broadcasted_iota(jnp.int32, (1, PAIR), 1) < DH
    keys = qkv_ref[:, PAIR : 2 * PAIR]
    values = qkv_ref[:, 2 * PAIR :]
    bias = bias_ref[...]
    zero = jnp.zeros((), BF16)
    picks = (low, jnp.logical_not(low))
    head_keys = [jnp.where(pick, keys, zero) for pick in picks]
    for tile in range(rows // ROWS):
        at = slice(tile * ROWS, (tile + 1) * ROWS)
        query = qkv_ref[at, :PAIR]
        grad = grad_ref[at, :]
        both = grad.astype(F32) * out_ref[at, :].astype(F32)
        query_grad = jnp.zeros((ROWS, PAIR), F32)
        key_grad = jnp.zeros((rows, PAIR), F32)
        value_grad = jnp.zeros((rows, PAIR), F32)
        for head in range(2):
            pick = picks[head]
            mine = jnp.where(pick, query, zero)
            mine_grad = jnp.where(pick, grad, zero)
            delta = jnp.sum(jnp.where(pick, both, 0.0), axis=1, keepdims=True)
            logs = log_ref[at, head * DH : head * DH + 1]
            prob = jnp.exp(product_back(mine, keys) + bias - logs)
            d_prob = product_back(mine_grad, values)
            d_scores = (prob * (d_prob - delta)).astype(BF16)
            query_grad = query_grad + product(d_scores, head_keys[head])
            key_grad = key_grad + row_product(d_scores, mine, F32)
            value_grad = value_grad + row_product(prob.astype(BF16), mine_grad, F32)
        result_ref[at, :PAIR] = (query_grad * DH**-0.5).astype(BF16)
        if tile == 0:
            key_acc[...] = key_grad
            value_acc[...] = value_grad
        else:
            key_acc[...] += key_grad
            value_acc[...] += value_grad
    result_ref[:, PAIR : 2 * PAIR] = key_acc[...].astype(BF16)
    result_ref[:, 2 * PAIR :] = value_acc[...].astype(BF16)


def attend_back(qkv, bias, out, logs, grad):
    rows = qkv.shape[0]
    pairs = qkv.shape[1] // (3 * PAIR)
    flops = 2 * 5 * 2 * pairs * rows * rows * DH
    wide = pl.BlockSpec((rows, 3 * PAIR), lambda i: (0, i))
    narrow = pl.BlockSpec((rows, PAIR), lambda i: (0, i))
    return pl.pallas_call(
        attend_back_kernel,
        grid=(pairs,),
        in_specs=[wide, pl.BlockSpec((1, rows), lambda i: (0, 0)), narrow, narrow, narrow],
        out_specs=wide,
        out_shape=jax.ShapeDtypeStruct(qkv.shape, BF16),
        scratch_shapes=[pltpu.VMEM((rows, PAIR), F32)] * 2,
        cost_estimate=pl.CostEstimate(
            flops=4 * flops, bytes_accessed=12 * rows * pairs * PAIR * 2,
            transcendentals=2 * pairs * rows * rows,
        ),
        name="attend_back",
    )(qkv, bias, out, logs, grad)


def normed_of(hidden):
    centred = hidden - jnp.mean(hidden, axis=-1, keepdims=True)
    spread = jnp.mean(centred * centred, axis=-1, keepdims=True)
    scale = lax.rsqrt(spread + norm_eps)
    return centred * scale, scale


def norm_back(grad, gain, unit, scale):
    inner = grad * gain
    return scale * (
        inner
        - jnp.mean(inner, axis=-1, keepdims=True)
        - unit * jnp.mean(inner * unit, axis=-1, keepdims=True)
    )


def weave(parts):
    lead = parts[0].shape[0]
    parts = [part.reshape(lead, -1, PAIR) for part in parts]
    return jnp.stack(parts, axis=2).reshape(lead, -1)


def unweave(woven):
    lead = woven.shape[0]
    woven = woven.reshape(lead, -1, 3, PAIR)
    return [woven[:, :, part].reshape(lead, -1) for part in range(3)]


def per_device(
    layer_in,
    lengths,
    out_grad,
    query_weight,
    key_weight,
    value_weight,
    out_weight,
    up_weight,
    down_weight,
    query_bias,
    value_bias,
    out_bias,
    up_bias,
    down_bias,
    norm_gain,
    norm_bias,
    final_gain,
    final_bias,
):
    fsdp = lax.axis_index("fsdp")
    plane, core = fsdp // 2, fsdp % 2
    high, low = lax.axis_index("ctx"), lax.axis_index("tp")
    planes = lax.axis_size("fsdp") // 2
    half = query_weight.shape[0]
    rows = layer_in.shape[1]
    width = layer_in.shape[2]
    heads_width = query_weight.shape[1]
    hidden = up_weight.shape[1]
    key = 2 * plane + low if planes == 4 else low
    order = functools.partial(turned_columns, key=key, width=half)

    qkv_shard = weave([query_weight, key_weight, value_weight])
    qkv_weight = gather_rows(qkv_shard)
    mine_in = order(lax.dynamic_index_in_dim(layer_in, low, 0, keepdims=False))
    own = to_turned(mine_in)
    other = to_core(own)
    x = jnp.concatenate([own, other], axis=0)
    vectors = to_first(jnp.concatenate([query_bias, value_bias, up_bias]))
    lengths_other = to_core(lengths)
    length = jnp.where(core == high, lengths, lengths_other)
    length = lax.dynamic_index_in_dim(length, low, 0, keepdims=False)
    out_up = gather_rows(jnp.concatenate([out_weight.T, up_weight], axis=1))
    out_t = out_up[:, :heads_width]
    up = out_up[:, heads_width:]
    down_t = gather_rows(down_weight.T)
    mine_grad = order(lax.dynamic_index_in_dim(out_grad, low, 0, keepdims=False))
    own_grad = to_turned(mine_grad)

    out_b, down_b, gain1, bias1, gain2, bias2 = order(
        jnp.stack([out_bias, down_bias, norm_gain, norm_bias, final_gain, final_bias])
    )
    query_b = vectors[:heads_width]
    value_b = vectors[heads_width : 2 * heads_width]
    up_b = vectors[2 * heads_width :]
    qkv_b = weave([query_b[None], jnp.zeros_like(query_b)[None], value_b[None]])
    scales = weave(
        [
            jnp.full((1, heads_width), DH**-0.5, F32),
            jnp.ones((1, heads_width), F32),
            jnp.ones((1, heads_width), F32),
        ]
    )
    places = lax.iota(jnp.int32, rows)
    own_places = core * rows + places
    other_places = (1 - core) * rows + places
    valid = jnp.concatenate([own_places, other_places]) < length
    bias = jnp.where(valid, 0.0, masked_score).astype(F32)[None, :]
    row_valid = (own_places < length).astype(F32)[:, None]

    qkv = ((product(x, qkv_weight) + qkv_b) * scales).astype(BF16)
    merged, logs = attend(qkv, bias)
    attn = product_back(merged, out_t)
    first = own.astype(F32) + attn[:rows] + to_core(attn[rows:].astype(BF16)).astype(F32) + out_b
    unit1, scale1 = normed_of(first)
    normed = unit1 * gain1 + bias1
    normed_own = normed.astype(BF16)
    normed_low = jnp.concatenate([normed_own, to_core(normed_own)], axis=0)
    upper = product(normed_low, up) + up_b
    cdf = 0.5 * lax.erfc(upper * -(0.5**0.5))
    activated = (upper * cdf).astype(BF16)
    slope = (cdf + upper * jnp.exp(-0.5 * upper * upper) * (2 * jnp.pi) ** -0.5).astype(BF16)
    ffn = product_back(activated, down_t)
    second = normed + ffn[:rows] + to_core(ffn[rows:].astype(BF16)).astype(F32) + down_b
    unit2, scale2 = normed_of(second)
    result = order((unit2 * gain2 + bias2).astype(BF16))
    result = to_turned(result)
    result_pair = to_low(result)
    layer_out = jnp.where(
        low == 0, jnp.stack([result, result_pair]), jnp.stack([result_pair, result])
    )

    cot = own_grad.astype(F32) * row_valid
    final_gain_grad = jnp.sum(cot * unit2, axis=0)
    final_bias_grad = jnp.sum(cot, axis=0)
    d_second = norm_back(cot, gain2, unit2, scale2)
    d_ffn_own = d_second.astype(BF16)
    down_bias_grad = jnp.sum(d_ffn_own.astype(F32), axis=0)
    d_ffn = jnp.concatenate([d_ffn_own, to_core(d_ffn_own)], axis=0)
    down_part = scatter_rows(lambda a, b: row_product(d_ffn[:, a:b], activated), half)
    d_upper = (product(d_ffn, down_t) * slope.astype(F32)).astype(BF16)
    up_bias_grad = jnp.sum(d_upper.astype(F32), axis=0)
    up_part = scatter_rows(lambda a, b: row_product(normed_low[:, a:b], d_upper), half)
    back = product_back(d_upper, up)
    d_normed = d_second + back[:rows] + to_core(back[rows:].astype(BF16)).astype(F32)
    norm_gain_grad = jnp.sum(d_normed * unit1, axis=0)
    norm_bias_grad = jnp.sum(d_normed, axis=0)
    d_first = norm_back(d_normed, gain1, unit1, scale1)
    d_attn_own = d_first.astype(BF16)
    out_bias_grad = jnp.sum(d_attn_own.astype(F32), axis=0)
    d_attn = jnp.concatenate([d_attn_own, to_core(d_attn_own)], axis=0)
    d_merged = product(d_attn, out_t, BF16)
    out_part = scatter_rows(lambda a, b: row_product(d_attn[:, a:b], merged), half)
    d_qkv = attend_back(qkv, bias, merged, logs, d_merged)
    qkv_bias_grad = jnp.sum(d_qkv.astype(F32), axis=0, keepdims=True)
    query_bias_grad, _, value_bias_grad = (part[0] for part in unweave(qkv_bias_grad))
    qkv_part = scatter_rows(lambda a, b: row_product(x[:, a:b], d_qkv), half)
    back = product_back(d_qkv, qkv_weight)
    total = d_first + back[:rows] + to_core(back[rows:].astype(BF16)).astype(F32)
    total = to_turned(order(total.astype(BF16)))
    total_pair = to_low(total)
    input_grad = jnp.where(
        low == 0, jnp.stack([total, total_pair]), jnp.stack([total_pair, total])
    ).astype(F32)

    down_grad = summed_high(down_part).T
    up_grad = summed_high(up_part)
    out_weight_grad = summed_high(out_part).T
    query_grad, key_grad, value_grad = unweave(summed_high(qkv_part))

    def spread(vector):
        empty = jnp.zeros_like(vector)
        return jnp.where(
            core == 0, jnp.concatenate([vector, empty]), jnp.concatenate([empty, vector])
        )

    features = order(
        jnp.stack(
            [
                out_bias_grad,
                down_bias_grad,
                norm_gain_grad,
                norm_bias_grad,
                final_gain_grad,
                final_bias_grad,
            ]
        )
    ).reshape(-1)
    small = summed_all(
        jnp.concatenate(
            [features, spread(query_bias_grad), spread(value_bias_grad), spread(up_bias_grad)]
        )
    )
    features = small[: 6 * width].reshape(6, width)
    at = 6 * width

    def mine(start, size):
        return lax.dynamic_slice(small, (start + low * size,), (size,))

    query_bias_grad = mine(at, heads_width)
    value_bias_grad = mine(at + 2 * heads_width, heads_width)
    up_bias_grad = mine(at + 4 * heads_width, hidden)
    return (
        layer_out,
        input_grad,
        query_grad,
        key_grad,
        value_grad,
        out_weight_grad,
        up_grad,
        down_grad,
        query_bias_grad,
        value_bias_grad,
        features[0],
        up_bias_grad,
        features[1],
        features[2],
        features[3],
        features[4],
        features[5],
    )


def solution(mesh):
    in_specs = (
        P("fsdp", "ctx", None),
        P("fsdp"),
        P("fsdp", "ctx", None),
        P("fsdp", "tp"),
        P("fsdp", "tp"),
        P("fsdp", "tp"),
        P("tp", "fsdp"),
        P("fsdp", "tp"),
        P("tp", "fsdp"),
        P("tp"),
        P("tp"),
        P(),
        P("tp"),
        P(),
        P(),
        P(),
        P(),
        P(),
    )
    out_specs = (
        P("fsdp", "ctx", None),
        P("fsdp", "ctx", None),
        P("fsdp", "tp"),
        P("fsdp", "tp"),
        P("fsdp", "tp"),
        P("tp", "fsdp"),
        P("fsdp", "tp"),
        P("tp", "fsdp"),
        P("tp"),
        P("tp"),
        P(),
        P("tp"),
        P(),
        P(),
        P(),
        P(),
        P(),
    )
    return jax.shard_map(
        per_device, mesh=mesh, in_specs=in_specs, out_specs=out_specs, check_vma=False
    )
```

```python
import functools

import jax
import jax.numpy as jnp
from jax import lax
from jax.experimental import pallas as pl
from jax.experimental.pallas import tpu as pltpu
from jax.sharding import PartitionSpec as P

DH = 64
PAIR = 2 * DH
ROWS = 256

norm_eps = 1e-05
masked_score = -1e30
BF16 = jnp.bfloat16
F32 = jnp.float32
AXES = ("fsdp", "ctx", "tp")


def send(value, target):
    fsdp, ctx, tp = (lax.axis_size(axis) for axis in AXES)
    pairs = []
    kept = 0
    for f in range(fsdp):
        for h in range(ctx):
            for t in range(tp):
                plane, core, high, low = target(f // 2, f % 2, h, t)
                source = (f * ctx + h) * tp + t
                place_of = ((2 * plane + core) * ctx + high) * tp + low
                if source == place_of:
                    kept += 1
                else:
                    pairs.append((source, place_of))
    moved = lax.ppermute(value, AXES, pairs)
    if not kept:
        return moved
    plane, core = lax.axis_index("fsdp") // 2, lax.axis_index("fsdp") % 2
    high, low = lax.axis_index("ctx"), lax.axis_index("tp")
    _, at_core, at_high, at_low = target(plane, core, high, low)
    stays = (at_core == core) & (at_high == high) & (at_low == low)
    return jnp.where(stays, value, moved)


def to_core(value):
    return send(value, lambda p, c, h, t: (p, 1 - c, h, t))


def to_x(value):
    return send(value, lambda p, c, h, t: (p ^ 1, c, h, t))


def to_y(value):
    return send(value, lambda p, c, h, t: (p ^ 2, c, h, t))


def to_high(value):
    return send(value, lambda p, c, h, t: (p, c, 1 - h, t))


def to_low(value):
    return send(value, lambda p, c, h, t: (p, c, h, 1 - t))


def to_turned(value):
    return send(value, lambda p, c, h, t: (p, h, c, t))


def to_first(value):
    return send(value, lambda p, c, h, t: (p, t, h, c))


def to_second(value):
    return send(value, lambda p, c, h, t: (p, t, h, 1 - c))


def from_second(value):
    return send(value, lambda p, c, h, t: (p, 1 - t, h, c))


def plane_groups():
    fsdp = lax.axis_size("fsdp")
    return [[2 * p + c for p in range(fsdp // 2)] for c in range(2)]


def sorted_pair(first, second):
    low = lax.axis_index("tp")
    ahead = jnp.where(low == 0, first, second)
    behind = jnp.where(low == 0, second, first)
    return ahead, behind


def after(value, *others):
    return lax.optimization_barrier((value,) + others)[0]


def place_kernel(key_ref, *refs, homes, half, spans, outs):
    pieces = refs[: len(homes)]
    wholes, marks = refs[-1 - outs : -1], refs[-1]
    key = key_ref[0]
    copies = []
    for piece, blocks in zip(pieces, homes):
        for at, block in enumerate(blocks):
            start = pl.multiple_of((key ^ block) * half, half)
            for whole, (column, width) in zip(wholes, spans):
                copies.append(
                    pltpu.make_async_copy(
                        piece.at[pl.ds(at * half, half), pl.ds(column, width)],
                        whole.at[pl.ds(start, half), :],
                        marks.at[len(copies)],
                    )
                )
    for copy in copies:
        copy.start()
    for copy in copies:
        copy.wait()


def place(key, pieces, homes, half, spans, wholes=()):
    anywhere = pl.BlockSpec(memory_space=pl.ANY)
    near = pl.BlockSpec(memory_space=pltpu.VMEM)
    count = len(spans) * sum(len(home) for home in homes)
    first = 1 + len(pieces)
    return pl.pallas_call(
        functools.partial(place_kernel, homes=homes, half=half, spans=spans, outs=len(spans)),
        in_specs=[pl.BlockSpec(memory_space=pltpu.SMEM)]
        + [near] * len(pieces)
        + [anywhere] * len(wholes),
        out_specs=[anywhere] * len(spans),
        out_shape=[jax.ShapeDtypeStruct((8 * half, width), BF16) for _, width in spans],
        scratch_shapes=[pltpu.SemaphoreType.DMA((count,))],
        input_output_aliases={first + i: i for i in range(len(wholes))},
        name="place",
    )(key, *pieces, *wholes)


class Gather:
    def __init__(self, shard):
        self.half = shard.shape[0]
        self.width = shard.shape[1]
        self.first = to_first(shard)
        self.second = to_second(shard)
        self.planes = lax.axis_size("fsdp") // 2
        self.arrived = (self.first, self.second)

    def near(self, *others):
        if self.planes != 4:
            unit = jnp.concatenate(sorted_pair(self.first, self.second), axis=0)
            self.whole = lax.all_gather(
                unit, "fsdp", axis=0, tiled=True, axis_index_groups=plane_groups()
            )
            return
        first, second = after(self.first, *others), after(self.second, *others)
        self.over_x = (to_x(first), to_x(second))
        self.over_y = (to_y(first), to_y(second))

    def far(self, key, spans):
        if self.planes != 4:
            return [[self.whole[:, a : a + n] for a, n in group] for group in spans]
        half = self.half
        sent = []
        for group in spans:
            start, stop = group[0][0], group[-1][0] + group[-1][1]
            first = to_y(self.over_x[0][:, start:stop])
            second = to_x(self.over_y[1][:, start:stop])
            sent.append((start, first, second))
        result = []
        pieces = (self.first, self.second) + self.over_x + self.over_y
        homes = tuple((block,) for block in range(6))
        for group, (start, first, second) in zip(spans, sent):
            wholes = place(key, pieces, homes, half, group)
            moved = [(a - start, n) for a, n in group]
            result.append(place(key, (first, second), ((6,), (7,)), half, moved, wholes))
        return result


def feature_rows(lefts, right):
    half = right.shape[0] // 2
    total = row_product(lefts[0][...], right[:half, :], F32)
    return total + row_product(lefts[1][...], right[half:, :], F32)


def far_kernel(at_ref, own_ref, other_ref, right_ref, first_ref, second_ref):
    half = first_ref.shape[0]
    total = feature_rows((own_ref, other_ref), right_ref).astype(BF16)
    first_ref[...] = total[:half]
    second_ref[...] = total[half:]


def near_kernel(
    at_ref, x_own, x_other, y_own, y_other, right_ref, first_ref, second_ref, x_ref, y_ref
):
    half = first_ref.shape[0]
    over_x = feature_rows((x_own, x_other), right_ref)
    x_ref[:half, :] = (over_x[:half] + first_ref[...].astype(F32)).astype(BF16)
    x_ref[half:, :] = over_x[half:].astype(BF16)
    over_y = feature_rows((y_own, y_other), right_ref)
    y_ref[:half, :] = over_y[:half].astype(BF16)
    y_ref[half:, :] = (over_y[half:] + second_ref[...].astype(F32)).astype(BF16)


def own_kernel(at_ref, own_ref, other_ref, right_ref, x_ref, y_ref, first_ref, second_ref):
    half = first_ref.shape[0]
    low = at_ref[1]
    total = feature_rows((own_ref, other_ref), right_ref)
    total = total + x_ref[...].astype(F32) + y_ref[...].astype(F32)
    total = total.astype(BF16)
    first_ref[...] = jnp.where(low == 0, total[:half], total[half:])
    second_ref[...] = jnp.where(low == 0, total[half:], total[:half])


def feature_call(kernel, name, at, lefts, right, extras, steps, outs):
    tokens, width = right.shape
    tile = min(width, 512)
    size = 2 * (lefts[0].shape[1] // 8)

    def left_spec(step):
        return pl.BlockSpec((tokens // 2, size), lambda i, at: (0, at[0] ^ step))

    def column_spec(rows):
        return pl.BlockSpec((rows, tile), lambda i, at: (0, i))

    operands, specs = [], []
    for step in steps:
        for left in lefts:
            operands.append(left)
            specs.append(left_spec(step))
    return pl.pallas_call(
        kernel,
        grid_spec=pltpu.PrefetchScalarGridSpec(
            num_scalar_prefetch=1,
            grid=(width // tile,),
            in_specs=specs + [column_spec(tokens)] + [column_spec(e.shape[0]) for e in extras],
            out_specs=[column_spec(rows) for rows in outs],
        ),
        out_shape=[jax.ShapeDtypeStruct((rows, width), BF16) for rows in outs],
        cost_estimate=pl.CostEstimate(
            flops=tokens * width, bytes_accessed=tokens * width, transcendentals=0
        ),
        name=name,
    )(at, *operands, right, *extras)


class Scatter:
    def __init__(self, lefts, right, half):
        self.half = half
        self.lefts = lefts
        self.right = right
        self.planes = lax.axis_size("fsdp") // 2
        plane, low = lax.axis_index("fsdp") // 2, lax.axis_index("tp")
        self.at = jnp.stack([plane, low]).astype(jnp.int32)
        if self.planes == 4:
            first, second = feature_call(
                far_kernel, "far_rows", self.at, lefts, right, (), (3,), (half, half)
            )
            self.far_first = to_y(first)
            self.far_second = to_x(second)

    def near(self, *others):
        if self.planes != 4:
            return
        half = self.half
        over_x, over_y = feature_call(
            near_kernel, "near_rows", self.at, self.lefts, after(self.right, *others),
            (self.far_first, self.far_second), (1, 2), (2 * half, 2 * half),
        )
        self.over_x = to_x(over_x)
        self.over_y = to_y(over_y)

    def own(self, *others):
        half = self.half
        right = after(self.right, *others)
        if self.planes != 4:
            mine = lax.psum_scatter(
                row_product(jnp.concatenate(self.lefts, axis=0), right), "fsdp",
                scatter_dimension=0, tiled=True, axis_index_groups=plane_groups(),
            )
            self.pair = sorted_pair(mine[:half], mine[half:])
        else:
            self.pair = feature_call(
                own_kernel, "own_rows", self.at, self.lefts, right,
                (self.over_x, self.over_y), (0,), (half, half),
            )
        self.landed = (to_first(self.pair[0]), from_second(self.pair[1]))

    def part(self):
        return added(*self.landed)


def added(one, other):
    return (one.astype(F32) + other.astype(F32)).astype(BF16)


def summed_high(part):
    return part.astype(F32) + to_high(part).astype(F32)


def summed_all(vector):
    fsdp = lax.axis_size("fsdp")
    if fsdp != 8:
        return lax.psum(vector, AXES)
    for step in (to_core, to_x, to_y, to_low, to_high):
        vector = vector + step(vector)
    return vector


def product(left, right, out=F32):
    return jnp.dot(left, right, preferred_element_type=F32).astype(out)


def product_back(left, right, out=F32):
    return lax.dot_general(
        left, right, (((1,), (1,)), ((), ())), preferred_element_type=F32
    ).astype(out)


def row_product(left, right, out=BF16):
    return lax.dot_general(
        left, right, (((0,), (0,)), ((), ())), preferred_element_type=F32
    ).astype(out)


def attend_kernel(qkv_ref, bias_ref, out_ref, log_ref):
    rows = qkv_ref.shape[0]
    low = lax.broadcasted_iota(jnp.int32, (1, PAIR), 1) < DH
    keys = qkv_ref[:, PAIR : 2 * PAIR]
    values = qkv_ref[:, 2 * PAIR :]
    bias = bias_ref[...]
    zero = jnp.zeros((), BF16)
    picks = (low, jnp.logical_not(low))
    head_values = [jnp.where(pick, values, zero) for pick in picks]
    for tile in range(rows // ROWS):
        at = slice(tile * ROWS, (tile + 1) * ROWS)
        query = qkv_ref[at, :PAIR]
        out = jnp.zeros((ROWS, PAIR), F32)
        logs = jnp.zeros((ROWS, PAIR), F32)
        for head in range(2):
            mine = jnp.where(picks[head], query, zero)
            scores = product_back(mine, keys) + bias
            top = jnp.max(scores, axis=1, keepdims=True)
            weights = jnp.exp(scores - top)
            total = jnp.sum(weights, axis=1, keepdims=True)
            out = out + product(weights.astype(BF16), head_values[head]) / total
            logs = jnp.where(picks[head], top + jnp.log(total), logs)
        out_ref[at, :] = out.astype(BF16)
        log_ref[at, :] = logs


def attend(qkv, bias):
    rows = qkv.shape[0]
    pairs = qkv.shape[1] // (3 * PAIR)
    flops = 2 * 2 * 2 * pairs * rows * rows * DH
    return pl.pallas_call(
        attend_kernel,
        grid=(pairs,),
        in_specs=[
            pl.BlockSpec((rows, 3 * PAIR), lambda i: (0, i)),
            pl.BlockSpec((1, rows), lambda i: (0, 0)),
        ],
        out_specs=[
            pl.BlockSpec((rows, PAIR), lambda i: (0, i)),
            pl.BlockSpec((rows, PAIR), lambda i: (0, i)),
        ],
        out_shape=[
            jax.ShapeDtypeStruct((rows, pairs * PAIR), BF16),
            jax.ShapeDtypeStruct((rows, pairs * PAIR), F32),
        ],
        cost_estimate=pl.CostEstimate(
            flops=flops // 64, bytes_accessed=rows * pairs * PAIR, transcendentals=0,
        ),
        name="attend",
    )(qkv, bias)


def attend_back_kernel(qkv_ref, bias_ref, out_ref, log_ref, grad_ref, result_ref, key_acc, value_acc):
    rows = qkv_ref.shape[0]
    low = lax.broadcasted_iota(jnp.int32, (1, PAIR), 1) < DH
    keys = qkv_ref[:, PAIR : 2 * PAIR]
    values = qkv_ref[:, 2 * PAIR :]
    bias = bias_ref[...]
    zero = jnp.zeros((), BF16)
    picks = (low, jnp.logical_not(low))
    head_keys = [jnp.where(pick, keys, zero) for pick in picks]
    for tile in range(rows // ROWS):
        at = slice(tile * ROWS, (tile + 1) * ROWS)
        query = qkv_ref[at, :PAIR]
        grad = grad_ref[at, :]
        both = grad.astype(F32) * out_ref[at, :].astype(F32)
        query_grad = jnp.zeros((ROWS, PAIR), F32)
        key_grad = jnp.zeros((rows, PAIR), F32)
        value_grad = jnp.zeros((rows, PAIR), F32)
        for head in range(2):
            pick = picks[head]
            mine = jnp.where(pick, query, zero)
            mine_grad = jnp.where(pick, grad, zero)
            delta = jnp.sum(jnp.where(pick, both, 0.0), axis=1, keepdims=True)
            logs = log_ref[at, head * DH : head * DH + 1]
            prob = jnp.exp(product_back(mine, keys) + bias - logs)
            d_prob = product_back(mine_grad, values)
            d_scores = (prob * (d_prob - delta)).astype(BF16)
            query_grad = query_grad + product(d_scores, head_keys[head])
            key_grad = key_grad + row_product(d_scores, mine, F32)
            value_grad = value_grad + row_product(prob.astype(BF16), mine_grad, F32)
        result_ref[at, :PAIR] = (query_grad * DH**-0.5).astype(BF16)
        if tile == 0:
            key_acc[...] = key_grad
            value_acc[...] = value_grad
        else:
            key_acc[...] += key_grad
            value_acc[...] += value_grad
    result_ref[:, PAIR : 2 * PAIR] = key_acc[...].astype(BF16)
    result_ref[:, 2 * PAIR :] = value_acc[...].astype(BF16)


def attend_back(qkv, bias, out, logs, grad):
    rows = qkv.shape[0]
    pairs = qkv.shape[1] // (3 * PAIR)
    flops = 2 * 5 * 2 * pairs * rows * rows * DH
    wide = pl.BlockSpec((rows, 3 * PAIR), lambda i: (0, i))
    narrow = pl.BlockSpec((rows, PAIR), lambda i: (0, i))
    return pl.pallas_call(
        attend_back_kernel,
        grid=(pairs,),
        in_specs=[wide, pl.BlockSpec((1, rows), lambda i: (0, 0)), narrow, narrow, narrow],
        out_specs=wide,
        out_shape=jax.ShapeDtypeStruct(qkv.shape, BF16),
        scratch_shapes=[pltpu.VMEM((rows, PAIR), F32)] * 2,
        cost_estimate=pl.CostEstimate(
            flops=flops // 64, bytes_accessed=rows * pairs * PAIR, transcendentals=0,
        ),
        name="attend_back",
    )(qkv, bias, out, logs, grad)


def normed_of(hidden):
    centred = hidden - jnp.mean(hidden, axis=-1, keepdims=True)
    spread = jnp.mean(centred * centred, axis=-1, keepdims=True)
    scale = lax.rsqrt(spread + norm_eps)
    return centred * scale, scale


def norm_back(grad, gain, unit, scale):
    inner = grad * gain
    return scale * (
        inner
        - jnp.mean(inner, axis=-1, keepdims=True)
        - unit * jnp.mean(inner * unit, axis=-1, keepdims=True)
    )


def weave(parts):
    lead = parts[0].shape[0]
    parts = [part.reshape(lead, -1, PAIR) for part in parts]
    return jnp.stack(parts, axis=2).reshape(lead, -1)


def unweave(woven):
    lead = woven.shape[0]
    woven = woven.reshape(lead, -1, 3, PAIR)
    return [woven[:, :, part].reshape(lead, -1) for part in range(3)]


def per_device(
    layer_in,
    lengths,
    out_grad,
    query_weight,
    key_weight,
    value_weight,
    out_weight,
    up_weight,
    down_weight,
    query_bias,
    value_bias,
    out_bias,
    up_bias,
    down_bias,
    norm_gain,
    norm_bias,
    final_gain,
    final_bias,
):
    fsdp = lax.axis_index("fsdp")
    plane, core = fsdp // 2, fsdp % 2
    high, low = lax.axis_index("ctx"), lax.axis_index("tp")
    planes = lax.axis_size("fsdp") // 2
    half = query_weight.shape[0]
    rows = layer_in.shape[1]
    width = layer_in.shape[2]
    heads_width = query_weight.shape[1]
    hidden = up_weight.shape[1]
    key = (2 * plane + low).astype(jnp.int32)[None]
    qkv_width = 3 * heads_width
    inner_gather = Gather(
        jnp.concatenate([weave([query_weight, key_weight, value_weight]), out_weight.T], axis=1)
    )
    mine_in = lax.dynamic_index_in_dim(layer_in, low, 0, keepdims=False)
    own = to_turned(mine_in)
    inner_gather.near()
    outer_shard = jnp.concatenate([up_weight, down_weight.T], axis=1)
    outer_gather = Gather(after(outer_shard, inner_gather.first, inner_gather.second))
    other = to_core(own)
    x = jnp.concatenate([own, other], axis=0)
    vectors = to_first(jnp.concatenate([query_bias, value_bias, up_bias]))
    lengths_other = to_core(lengths)
    length = jnp.where(core == high, lengths, lengths_other)
    length = lax.dynamic_index_in_dim(length, low, 0, keepdims=False)
    ((qkv_weight, out_t),) = inner_gather.far(
        key, (((0, qkv_width), (qkv_width, heads_width)),)
    )
    if planes == 4:
        outer_gather.near(*inner_gather.over_x, *inner_gather.over_y)
    else:
        outer_gather.near()
    mine_grad = lax.dynamic_index_in_dim(out_grad, low, 0, keepdims=False)
    own_grad = to_turned(after(mine_grad, own))
    x = after(x, *outer_gather.arrived)

    out_b, down_b, gain1, bias1, gain2, bias2 = (
        out_bias, down_bias, norm_gain, norm_bias, final_gain, final_bias
    )
    query_b = vectors[:heads_width]
    value_b = vectors[heads_width : 2 * heads_width]
    up_b = vectors[2 * heads_width :]
    qkv_b = weave([query_b[None], jnp.zeros_like(query_b)[None], value_b[None]])
    scales = weave(
        [
            jnp.full((1, heads_width), DH**-0.5, F32),
            jnp.ones((1, heads_width), F32),
            jnp.ones((1, heads_width), F32),
        ]
    )
    places = lax.iota(jnp.int32, rows)
    own_places = core * rows + places
    other_places = (1 - core) * rows + places
    valid = jnp.concatenate([own_places, other_places]) < length
    bias = jnp.where(valid, 0.0, masked_score).astype(F32)[None, :]
    row_valid = (own_places < length).astype(F32)[:, None]

    qkv = ((product(x, qkv_weight) + qkv_b) * scales).astype(BF16)
    merged, logs = attend(qkv, bias)
    if planes == 4:
        merged = after(merged, own_grad, *outer_gather.over_x, *outer_gather.over_y)
    (up,), (down_t,) = outer_gather.far(key, (((0, hidden),), ((hidden, hidden),)))
    attn_other = to_core(product_back(merged[rows:], out_t, BF16))
    attn = product_back(merged[:rows], out_t)
    first = own.astype(F32) + attn + attn_other.astype(F32) + out_b
    unit1, scale1 = normed_of(first)
    normed = unit1 * gain1 + bias1
    normed_own = normed.astype(BF16)
    normed_other = to_core(normed_own)
    normed_low = jnp.concatenate([normed_own, normed_other], axis=0)
    upper = product(normed_low, up) + up_b
    cdf = 0.5 + 0.5 * lax.erf(upper * 0.5**0.5)
    activated = (upper * cdf).astype(BF16)
    slope = (cdf + upper * jnp.exp(-0.5 * upper * upper) * (2 * jnp.pi) ** -0.5).astype(BF16)
    activated, slope = lax.optimization_barrier((activated, slope))
    ffn_other = to_core(product_back(activated[rows:], down_t, BF16))
    ffn = product_back(activated[:rows], down_t)
    second = normed + ffn + ffn_other.astype(F32) + down_b
    unit2, scale2 = normed_of(second)
    result = (unit2 * gain2 + bias2).astype(BF16)
    result = to_turned(result)
    result_pair = to_low(result)
    layer_out = jnp.where(
        low == 0, jnp.stack([result, result_pair]), jnp.stack([result_pair, result])
    )

    cot = own_grad.astype(F32) * row_valid
    final_gain_grad = jnp.sum(cot * unit2, axis=0)
    final_bias_grad = jnp.sum(cot, axis=0)
    d_second = norm_back(cot, gain2, unit2, scale2)
    d_ffn_own = d_second.astype(BF16)
    down_bias_grad = jnp.sum(d_ffn_own.astype(F32), axis=0)
    d_ffn_other = to_core(d_ffn_own)
    d_ffn = jnp.concatenate([d_ffn_own, d_ffn_other], axis=0)
    down_scatter = Scatter((d_ffn_own, d_ffn_other), activated, half)
    d_upper = (product(d_ffn, down_t) * slope.astype(F32)).astype(BF16)
    down_scatter.near()
    up_bias_grad = jnp.sum(d_upper.astype(F32), axis=0)
    back_other = to_core(product_back(d_upper[rows:], up, BF16))
    back = product_back(d_upper[:rows], up)
    d_normed = d_second + back + back_other.astype(F32)
    up_scatter = Scatter((normed_own, normed_other), d_upper, half)
    norm_gain_grad = jnp.sum(d_normed * unit1, axis=0)
    norm_bias_grad = jnp.sum(d_normed, axis=0)
    d_first = norm_back(d_normed, gain1, unit1, scale1)
    d_attn_own = d_first.astype(BF16)
    out_bias_grad = jnp.sum(d_attn_own.astype(F32), axis=0)
    d_attn_other = to_core(d_attn_own)
    d_attn = jnp.concatenate([d_attn_own, d_attn_other], axis=0)
    up_scatter.near()
    down_scatter.own()
    d_merged = product(d_attn, out_t, BF16)
    out_scatter = Scatter((d_attn_own, d_attn_other), merged, half)
    if planes == 4:
        d_merged = after(d_merged, *down_scatter.pair, out_scatter.far_first)
    d_qkv = attend_back(qkv, bias, merged, logs, d_merged)
    out_scatter.near()
    back_other = to_core(product_back(d_qkv[rows:], qkv_weight, BF16))
    back = product_back(d_qkv[:rows], qkv_weight)
    total = d_first + back + back_other.astype(F32)
    total = to_turned(total.astype(BF16))
    qkv_scatter = Scatter((own, other), d_qkv, half)
    up_scatter.own()
    out_scatter.own()
    qkv_scatter.near()
    qkv_bias_grad = jnp.sum(d_qkv.astype(F32), axis=0, keepdims=True)
    query_bias_grad, _, value_bias_grad = (part[0] for part in unweave(qkv_bias_grad))
    down_part = down_scatter.part()
    up_part = up_scatter.part()
    out_part = out_scatter.part()
    total_pair = to_low(total)
    input_grad = jnp.where(
        low == 0, jnp.stack([total, total_pair]), jnp.stack([total_pair, total])
    ).astype(F32)
    qkv_scatter.own()
    qkv_part = qkv_scatter.part()

    down_grad = summed_high(down_part).T
    up_grad = summed_high(up_part)
    out_weight_grad = summed_high(out_part).T
    query_grad, key_grad, value_grad = unweave(summed_high(qkv_part))

    def spread(vector):
        empty = jnp.zeros_like(vector)
        return jnp.where(
            core == 0, jnp.concatenate([vector, empty]), jnp.concatenate([empty, vector])
        )

    features = (
        jnp.stack(
            [
                out_bias_grad,
                down_bias_grad,
                norm_gain_grad,
                norm_bias_grad,
                final_gain_grad,
                final_bias_grad,
            ]
        )
    ).reshape(-1)
    small = summed_all(
        jnp.concatenate(
            [features, spread(query_bias_grad), spread(value_bias_grad), spread(up_bias_grad)]
        )
    )
    features = small[: 6 * width].reshape(6, width)
    at = 6 * width

    def mine(start, size):
        return lax.dynamic_slice(small, (start + low * size,), (size,))

    query_bias_grad = mine(at, heads_width)
    value_bias_grad = mine(at + 2 * heads_width, heads_width)
    up_bias_grad = mine(at + 4 * heads_width, hidden)
    return (
        layer_out,
        input_grad,
        query_grad,
        key_grad,
        value_grad,
        out_weight_grad,
        up_grad,
        down_grad,
        query_bias_grad,
        value_bias_grad,
        features[0],
        up_bias_grad,
        features[1],
        features[2],
        features[3],
        features[4],
        features[5],
    )


def solution(mesh):
    in_specs = (
        P("fsdp", "ctx", None),
        P("fsdp"),
        P("fsdp", "ctx", None),
        P("fsdp", "tp"),
        P("fsdp", "tp"),
        P("fsdp", "tp"),
        P("tp", "fsdp"),
        P("fsdp", "tp"),
        P("tp", "fsdp"),
        P("tp"),
        P("tp"),
        P(),
        P("tp"),
        P(),
        P(),
        P(),
        P(),
        P(),
    )
    out_specs = (
        P("fsdp", "ctx", None),
        P("fsdp", "ctx", None),
        P("fsdp", "tp"),
        P("fsdp", "tp"),
        P("fsdp", "tp"),
        P("tp", "fsdp"),
        P("fsdp", "tp"),
        P("tp", "fsdp"),
        P("tp"),
        P("tp"),
        P(),
        P("tp"),
        P(),
        P(),
        P(),
        P(),
        P(),
    )
    return jax.shard_map(
        per_device, mesh=mesh, in_specs=in_specs, out_specs=out_specs, check_vma=False
    )
```

```python
import functools

import jax
import jax.numpy as jnp
from jax import lax
from jax.experimental import pallas as pl
from jax.experimental.pallas import tpu as pltpu
from jax.sharding import PartitionSpec as P

DH = 64
PAIR = 2 * DH
ROWS = 256

norm_eps = 1e-05
masked_score = -1e30
BF16 = jnp.bfloat16
F32 = jnp.float32
AXES = ("fsdp", "ctx", "tp")


def send(value, target):
    fsdp, ctx, tp = (lax.axis_size(axis) for axis in AXES)
    pairs = []
    kept = 0
    for f in range(fsdp):
        for h in range(ctx):
            for t in range(tp):
                plane, core, high, low = target(f // 2, f % 2, h, t)
                source = (f * ctx + h) * tp + t
                place_of = ((2 * plane + core) * ctx + high) * tp + low
                if source == place_of:
                    kept += 1
                else:
                    pairs.append((source, place_of))
    moved = lax.ppermute(value, AXES, pairs)
    if not kept:
        return moved
    plane, core = lax.axis_index("fsdp") // 2, lax.axis_index("fsdp") % 2
    high, low = lax.axis_index("ctx"), lax.axis_index("tp")
    _, at_core, at_high, at_low = target(plane, core, high, low)
    stays = (at_core == core) & (at_high == high) & (at_low == low)
    return jnp.where(stays, value, moved)


def to_core(value):
    return send(value, lambda p, c, h, t: (p, 1 - c, h, t))


def to_x(value):
    return send(value, lambda p, c, h, t: (p ^ 1, c, h, t))


def to_y(value):
    return send(value, lambda p, c, h, t: (p ^ 2, c, h, t))


def to_high(value):
    return send(value, lambda p, c, h, t: (p, c, 1 - h, t))


def to_low(value):
    return send(value, lambda p, c, h, t: (p, c, h, 1 - t))


def to_turned(value):
    return send(value, lambda p, c, h, t: (p, h, c, t))


def to_first(value):
    return send(value, lambda p, c, h, t: (p, t, h, c))


def to_second(value):
    return send(value, lambda p, c, h, t: (p, t, h, 1 - c))


def from_second(value):
    return send(value, lambda p, c, h, t: (p, 1 - t, h, c))


def plane_groups():
    fsdp = lax.axis_size("fsdp")
    return [[2 * p + c for p in range(fsdp // 2)] for c in range(2)]


def sorted_pair(first, second):
    low = lax.axis_index("tp")
    ahead = jnp.where(low == 0, first, second)
    behind = jnp.where(low == 0, second, first)
    return ahead, behind


def after(value, *others):
    return lax.optimization_barrier((value,) + others)[0]


def place_kernel(key_ref, *refs, homes, half, spans, outs):
    pieces = refs[: len(homes)]
    wholes, marks = refs[-1 - outs : -1], refs[-1]
    key = key_ref[0]
    copies = []
    for piece, blocks in zip(pieces, homes):
        for at, block in enumerate(blocks):
            start = pl.multiple_of((key ^ block) * half, half)
            for whole, (column, width) in zip(wholes, spans):
                copies.append(
                    pltpu.make_async_copy(
                        piece.at[pl.ds(at * half, half), pl.ds(column, width)],
                        whole.at[pl.ds(start, half), :],
                        marks.at[len(copies)],
                    )
                )
    for copy in copies:
        copy.start()
    for copy in copies:
        copy.wait()


def place(key, pieces, homes, half, spans, wholes=()):
    anywhere = pl.BlockSpec(memory_space=pl.ANY)
    near = pl.BlockSpec(memory_space=pltpu.VMEM)
    count = len(spans) * sum(len(home) for home in homes)
    first = 1 + len(pieces)
    return pl.pallas_call(
        functools.partial(place_kernel, homes=homes, half=half, spans=spans, outs=len(spans)),
        in_specs=[pl.BlockSpec(memory_space=pltpu.SMEM)]
        + [near] * len(pieces)
        + [anywhere] * len(wholes),
        out_specs=[anywhere] * len(spans),
        out_shape=[jax.ShapeDtypeStruct((8 * half, width), BF16) for _, width in spans],
        scratch_shapes=[pltpu.SemaphoreType.DMA((count,))],
        input_output_aliases={first + i: i for i in range(len(wholes))},
        name="place",
    )(key, *pieces, *wholes)


class Gather:
    def __init__(self, shard):
        self.half = shard.shape[0]
        self.width = shard.shape[1]
        self.first = to_first(shard)
        self.second = to_second(shard)
        self.planes = lax.axis_size("fsdp") // 2
        self.arrived = (self.first, self.second)

    def near(self, *others):
        if self.planes != 4:
            unit = jnp.concatenate(sorted_pair(self.first, self.second), axis=0)
            self.whole = lax.all_gather(
                unit, "fsdp", axis=0, tiled=True, axis_index_groups=plane_groups()
            )
            return
        first, second = after(self.first, *others), after(self.second, *others)
        self.over_x = (to_x(first), to_x(second))
        self.over_y = (to_y(first), to_y(second))

    def far(self, spans):
        self.spans = spans
        self.sent = []
        for group in spans if self.planes == 4 else ():
            start, stop = group[0][0], group[-1][0] + group[-1][1]
            first, second = self.over_x[0], self.over_y[1]
            if stop - start != self.width:
                first, second = first[:, start:stop], second[:, start:stop]
            first, second = to_y(first), to_x(second)
            self.sent.append((start, first, second))

    def last(self):
        return self.sent[-1][1:] if self.planes == 4 else ()

    def placed(self, key, index):
        group = self.spans[index]
        if self.planes != 4:
            return [self.whole[:, a : a + n] for a, n in group]
        half = self.half
        pieces = (self.first, self.second) + self.over_x + self.over_y
        homes = tuple((block,) for block in range(6))
        start, first, second = self.sent[index]
        wholes = place(key, pieces, homes, half, group)
        moved = [(a - start, n) for a, n in group]
        return place(key, (first, second), ((6,), (7,)), half, moved, wholes)


TAIL = 16


def rows_kernel(at_ref, *refs, starts, half, tail, extra):
    count = len(starts) - 1
    lefts, rights = refs[: 2 * count], refs[2 * count : 3 * count]
    outs, turned = refs[3 * count + extra : -1], refs[-1]
    place_of = pl.program_id(0)
    tokens = turned.shape[1] // 2
    blocks = len(outs)
    plane, low = at_ref[0], at_ref[1]
    if tail:

        @pl.when(place_of == 0)
        def _():
            row = lax.broadcasted_iota(jnp.int32, (tail, 2 * tokens), 0)
            turned[blocks * half :, :] = (row == 0).astype(F32).astype(BF16)

    for source in range(count):

        @pl.when(place_of == starts[source])
        def _(source=source):
            for block in range(blocks):
                step, side = block // 2, block % 2
                start = (2 * (plane ^ step) + (side ^ low)) * half
                start = pl.multiple_of(start, half)
                for part in range(2):
                    left = lefts[2 * source + part][:, pl.ds(start, half)]
                    turned[
                        block * half : (block + 1) * half, part * tokens : (part + 1) * tokens
                    ] = left.T

        @pl.when((place_of >= starts[source]) & (place_of < starts[source + 1]))
        def _(source=source):
            total = product(turned[...], rights[source][...])
            last = total[blocks * half :]
            if extra:
                last = last + refs[3 * count][...]
            total, last = total.astype(BF16), last.astype(BF16)
            for block, out in enumerate(outs):
                out[:half, :] = total[block * half : (block + 1) * half]
                if tail:
                    out[half:, :] = last


def row_blocks(at, sources, half, tail, extra):
    tile = 512
    starts = [0]
    for _, _, right in sources:
        starts.append(starts[-1] + right.shape[1] // tile)
    width = starts[-1] * tile
    tokens = sources[0][2].shape[0]
    features = sources[0][0].shape[1]
    blocks = features // half

    def right_spec(start, stop):
        return pl.BlockSpec(
            (tokens, tile), lambda i, at: (0, jnp.clip(i - start, 0, stop - start - 1))
        )

    operands, specs = [], []
    for own, other, _ in sources:
        operands += [own, other]
        specs += [pl.BlockSpec((tokens // 2, features), lambda i, at: (0, 0))] * 2
    for source, (_, _, right) in enumerate(sources):
        operands.append(right)
        specs.append(right_spec(starts[source], starts[source + 1]))
    if extra is not None:
        operands.append(extra)
        specs.append(pl.BlockSpec((tail, tile), lambda i, at: (0, i)))
    return pl.pallas_call(
        functools.partial(
            rows_kernel, starts=tuple(starts), half=half, tail=tail, extra=int(extra is not None)
        ),
        grid_spec=pltpu.PrefetchScalarGridSpec(
            num_scalar_prefetch=1,
            grid=(starts[-1],),
            in_specs=specs,
            out_specs=[pl.BlockSpec((half + tail, tile), lambda i, at: (0, i))] * blocks,
            scratch_shapes=[pltpu.VMEM((features + tail, tokens), BF16)],
        ),
        out_shape=[jax.ShapeDtypeStruct((half + tail, width), BF16)] * blocks,
        cost_estimate=cheap(tokens * width),
        name="row_blocks",
    )(at, *operands)


def cheap(size):
    return pl.CostEstimate(flops=size, bytes_accessed=size // 4, transcendentals=0)


class Scatter:
    def __init__(self, sources, half, tail=0, extra=None):
        self.planes = lax.axis_size("fsdp") // 2
        plane, low = lax.axis_index("fsdp") // 2, lax.axis_index("tp")
        if self.planes == 4:
            at = jnp.stack([plane, low]).astype(jnp.int32)
            self.blocks = row_blocks(at, sources, half, tail, extra)
            self.far_first = to_y(self.blocks[6])
            self.far_second = to_x(self.blocks[7])
            self.x_second = to_x(self.blocks[3])
            self.y_first = to_y(self.blocks[4])
        else:
            whole = jnp.concatenate(
                [
                    row_product(jnp.concatenate([own, other], axis=0), right)
                    for own, other, right in sources
                ],
                axis=1,
            )
            mine = lax.psum_scatter(
                whole, "fsdp", scatter_dimension=0, tiled=True, axis_index_groups=plane_groups()
            )
            self.blocks = sorted_pair(mine[:half], mine[half:])

    def near(self, *others):
        if self.planes != 4:
            return ()
        blocks = self.blocks
        if others:
            blocks = lax.optimization_barrier(tuple(blocks) + others)[: len(blocks)]
        sent = (added(blocks[2], self.far_first), added(blocks[5], self.far_second))
        sent = lax.optimization_barrier(sent)
        self.x_first = to_x(sent[0])
        self.y_second = to_y(sent[1])
        return sent

    def early(self):
        return (self.x_second, self.y_first) if self.planes == 4 else ()

    def own(self, *others):
        blocks = self.blocks
        if others:
            blocks = lax.optimization_barrier(tuple(blocks) + others)[: len(blocks)]
        first, second = blocks[0].astype(F32), blocks[1].astype(F32)
        if self.planes == 4:
            first = first + self.x_first.astype(F32) + self.y_first.astype(F32)
            second = second + self.x_second.astype(F32) + self.y_second.astype(F32)
        pair = lax.optimization_barrier((first.astype(BF16), second.astype(BF16)))
        self.landed = (to_first(pair[0]), from_second(pair[1]))
        return pair

    def part(self, *others):
        return added(after(self.landed[0], *others), self.landed[1])


def column_call(body, name, operands, weight, extras, outs, tile):
    width = weight.shape[1]

    def column_spec(rows):
        return pl.BlockSpec((rows, tile), lambda i: (0, i))

    return pl.pallas_call(
        body,
        grid=(width // tile,),
        in_specs=[pl.BlockSpec(left.shape, lambda i: (0, 0)) for left in operands]
        + [column_spec(array.shape[0]) for array in (weight,) + extras],
        out_specs=[column_spec(rows) for rows, _ in outs],
        out_shape=[jax.ShapeDtypeStruct((rows, width), kind) for rows, kind in outs],
        cost_estimate=cheap(weight.size),
        name=name,
    )(*operands, weight, *extras)


def up_kernel(own_ref, other_ref, weight_ref, bias_ref, active_ref, slope_ref):
    rows = own_ref.shape[0]
    for side, left in enumerate((own_ref, other_ref)):
        at = slice(side * rows, (side + 1) * rows)
        upper = product(left[...], weight_ref[...]) + bias_ref[...]
        cdf = 0.5 + 0.5 * lax.erf(upper * 0.5**0.5)
        active_ref[at, :] = (upper * cdf).astype(BF16)
        density = jnp.exp(upper * upper * -0.5) * (2 * jnp.pi) ** -0.5
        slope_ref[at, :] = (cdf + upper * density).astype(BF16)


def added(one, other):
    return (one.astype(F32) + other.astype(F32)).astype(BF16)


def summed(part, other):
    return part.astype(F32) + other.astype(F32)


def product(left, right, out=F32):
    return jnp.dot(left, right, preferred_element_type=F32).astype(out)


def product_back(left, right, out=F32):
    return lax.dot_general(
        left, right, (((1,), (1,)), ((), ())), preferred_element_type=F32
    ).astype(out)


def row_product(left, right, out=BF16):
    return lax.dot_general(
        left, right, (((0,), (0,)), ((), ())), preferred_element_type=F32
    ).astype(out)


def attend_kernel(qkv_ref, bias_ref, out_ref, log_ref):
    rows = qkv_ref.shape[0]
    low = lax.broadcasted_iota(jnp.int32, (1, PAIR), 1) < DH
    keys = qkv_ref[:, PAIR : 2 * PAIR]
    values = qkv_ref[:, 2 * PAIR :]
    bias = bias_ref[...]
    zero = jnp.zeros((), BF16)
    picks = (low, jnp.logical_not(low))
    head_values = [jnp.where(pick, values, zero) for pick in picks]
    for tile in range(rows // ROWS):
        at = slice(tile * ROWS, (tile + 1) * ROWS)
        query = qkv_ref[at, :PAIR]
        out = jnp.zeros((ROWS, PAIR), F32)
        logs = jnp.zeros((ROWS, PAIR), F32)
        for head in range(2):
            mine = jnp.where(picks[head], query, zero)
            scores = product_back(mine, keys) + bias
            top = jnp.max(scores, axis=1, keepdims=True)
            weights = jnp.exp(scores - top)
            total = jnp.sum(weights, axis=1, keepdims=True)
            out = out + product(weights.astype(BF16), head_values[head]) / total
            logs = jnp.where(picks[head], top + jnp.log(total), logs)
        out_ref[at, :] = out.astype(BF16)
        log_ref[at, :] = logs


def attend(qkv, bias):
    rows = qkv.shape[0]
    pairs = qkv.shape[1] // (3 * PAIR)
    flops = 2 * 2 * 2 * pairs * rows * rows * DH
    return pl.pallas_call(
        attend_kernel,
        grid=(pairs,),
        in_specs=[
            pl.BlockSpec((rows, 3 * PAIR), lambda i: (0, i)),
            pl.BlockSpec((1, rows), lambda i: (0, 0)),
        ],
        out_specs=[
            pl.BlockSpec((rows, PAIR), lambda i: (0, i)),
            pl.BlockSpec((rows, PAIR), lambda i: (0, i)),
        ],
        out_shape=[
            jax.ShapeDtypeStruct((rows, pairs * PAIR), BF16),
            jax.ShapeDtypeStruct((rows, pairs * PAIR), F32),
        ],
        cost_estimate=pl.CostEstimate(
            flops=flops // 64, bytes_accessed=rows * pairs * PAIR, transcendentals=0,
        ),
        name="attend",
    )(qkv, bias)


def attend_back_kernel(
    qkv_ref, bias_ref, out_ref, log_ref, grad_ref, result_ref, key_acc, value_acc
):
    rows = qkv_ref.shape[0]
    low = lax.broadcasted_iota(jnp.int32, (1, PAIR), 1) < DH
    keys = qkv_ref[:, PAIR : 2 * PAIR]
    values = qkv_ref[:, 2 * PAIR :]
    bias = bias_ref[...]
    zero = jnp.zeros((), BF16)
    picks = (low, jnp.logical_not(low))
    head_keys = [jnp.where(pick, keys, zero) for pick in picks]
    for tile in range(rows // ROWS):
        at = slice(tile * ROWS, (tile + 1) * ROWS)
        query = qkv_ref[at, :PAIR]
        grad = grad_ref[at, :]
        both = grad.astype(F32) * out_ref[at, :].astype(F32)
        query_grad = jnp.zeros((ROWS, PAIR), F32)
        key_grad = jnp.zeros((rows, PAIR), F32)
        value_grad = jnp.zeros((rows, PAIR), F32)
        for head in range(2):
            pick = picks[head]
            mine = jnp.where(pick, query, zero)
            mine_grad = jnp.where(pick, grad, zero)
            delta = jnp.sum(jnp.where(pick, both, 0.0), axis=1, keepdims=True)
            logs = log_ref[at, head * DH : head * DH + 1]
            prob = jnp.exp(product_back(mine, keys) + bias - logs)
            d_prob = product_back(mine_grad, values)
            d_scores = (prob * (d_prob - delta)).astype(BF16)
            query_grad = query_grad + product(d_scores, head_keys[head])
            key_grad = key_grad + row_product(d_scores, mine, F32)
            value_grad = value_grad + row_product(prob.astype(BF16), mine_grad, F32)
        query_grad = query_grad * DH**-0.5
        result_ref[at, :PAIR] = query_grad.astype(BF16)
        if tile == 0:
            key_acc[...] = key_grad
            value_acc[...] = value_grad
        else:
            key_acc[...] += key_grad
            value_acc[...] += value_grad
    result_ref[:, PAIR : 2 * PAIR] = key_acc[...].astype(BF16)
    result_ref[:, 2 * PAIR :] = value_acc[...].astype(BF16)


def attend_back(qkv, bias, out, logs, grad, pairs, begin, into=()):
    rows = qkv.shape[0]
    wide = pl.BlockSpec((rows, 3 * PAIR), lambda i: (0, i + begin))
    narrow = pl.BlockSpec((rows, PAIR), lambda i: (0, i + begin))

    def kernel(*refs):
        attend_back_kernel(*refs[:5], *refs[5 + len(into) :])

    return pl.pallas_call(
        kernel,
        grid=(pairs,),
        in_specs=[wide, pl.BlockSpec((1, rows), lambda i: (0, 0)), narrow, narrow, narrow]
        + [pl.BlockSpec(memory_space=pl.ANY)] * len(into),
        out_specs=wide,
        out_shape=jax.ShapeDtypeStruct(qkv.shape, BF16),
        scratch_shapes=[pltpu.VMEM((rows, PAIR), F32)] * 2,
        input_output_aliases={5: 0} if into else {},
        cost_estimate=cheap(rows * rows),
        name="attend_back",
    )(qkv, bias, out, logs, grad, *into)


def normed_of(hidden):
    centred = hidden - jnp.mean(hidden, axis=-1, keepdims=True)
    spread = jnp.mean(centred * centred, axis=-1, keepdims=True)
    scale = lax.rsqrt(spread + norm_eps)
    return centred * scale, scale


def norm_back(grad, gain, unit, scale):
    inner = grad * gain
    return scale * (
        inner
        - jnp.mean(inner, axis=-1, keepdims=True)
        - unit * jnp.mean(inner * unit, axis=-1, keepdims=True)
    )


def weave(parts):
    lead = parts[0].shape[0]
    parts = [part.reshape(lead, -1, PAIR) for part in parts]
    return jnp.stack(parts, axis=2).reshape(lead, -1)


def unweave(woven):
    lead = woven.shape[0]
    woven = woven.reshape(lead, -1, 3, PAIR)
    return [woven[:, :, part].reshape(lead, -1) for part in range(3)]


def per_device(
    layer_in,
    lengths,
    out_grad,
    query_weight,
    key_weight,
    value_weight,
    out_weight,
    up_weight,
    down_weight,
    query_bias,
    value_bias,
    out_bias,
    up_bias,
    down_bias,
    norm_gain,
    norm_bias,
    final_gain,
    final_bias,
):
    fsdp = lax.axis_index("fsdp")
    plane, core = fsdp // 2, fsdp % 2
    high, low = lax.axis_index("ctx"), lax.axis_index("tp")
    planes = lax.axis_size("fsdp") // 2
    half = query_weight.shape[0]
    rows = layer_in.shape[1]
    width = layer_in.shape[2]
    heads_width = query_weight.shape[1]
    hidden = up_weight.shape[1]
    key = (2 * plane + low).astype(jnp.int32)[None]
    qkv_width = 3 * heads_width
    inner_gather = Gather(
        jnp.concatenate([weave([query_weight, key_weight, value_weight]), out_weight.T], axis=1)
    )
    mine_in = lax.dynamic_index_in_dim(layer_in, low, 0, keepdims=False)
    own = to_turned(mine_in)
    length = lax.dynamic_index_in_dim(to_turned(lengths), low, 0, keepdims=False)
    inner_gather.near()
    outer_shard = jnp.concatenate([up_weight, down_weight.T], axis=1)
    outer_gather = Gather(after(outer_shard, inner_gather.first, inner_gather.second))
    inner_gather.far((((0, qkv_width), (qkv_width, heads_width)),))
    arrived = inner_gather.last()
    other = to_core(after(own, *arrived))
    vectors = to_first(after(jnp.concatenate([query_bias, value_bias, up_bias]), own, *arrived))
    if planes == 4:
        outer_gather.near(*inner_gather.over_x, *inner_gather.over_y)
    else:
        outer_gather.near()
    mine_grad = lax.dynamic_index_in_dim(out_grad, low, 0, keepdims=False)
    own_grad = to_turned(after(mine_grad, own))
    qkv_weight, out_t = inner_gather.placed(key, 0)
    own = after(own, *outer_gather.arrived)

    out_b, down_b, gain1, bias1, gain2, bias2 = (
        out_bias, down_bias, norm_gain, norm_bias, final_gain, final_bias
    )
    query_b = vectors[:heads_width]
    value_b = vectors[heads_width : 2 * heads_width]
    up_b = vectors[2 * heads_width :]
    qkv_b = weave([query_b[None], jnp.zeros_like(query_b)[None], value_b[None]])
    scales = weave(
        [
            jnp.full((1, heads_width), DH**-0.5, F32),
            jnp.ones((1, heads_width), F32),
            jnp.ones((1, heads_width), F32),
        ]
    )
    places = lax.iota(jnp.int32, rows)
    own_places = core * rows + places
    other_places = (1 - core) * rows + places
    valid = jnp.concatenate([own_places, other_places]) < length
    bias = jnp.where(valid, 0.0, masked_score).astype(F32)[None, :]
    row_valid = (own_places < length).astype(F32)[:, None]

    x = jnp.concatenate([own, other], axis=0)
    qkv = ((product(x, qkv_weight) + qkv_b) * scales).astype(BF16)
    merged, logs = attend(qkv, bias)
    if planes == 4:
        merged = after(merged, own_grad, *outer_gather.over_x, *outer_gather.over_y)
    outer_gather.far((((0, hidden), (hidden, hidden)),))
    attn_other = to_core(product_back(merged[rows:], out_t, BF16))
    attn = product_back(merged[:rows], out_t)
    first = own.astype(F32) + attn + attn_other.astype(F32) + out_b
    unit1, scale1 = normed_of(first)
    normed = unit1 * gain1 + bias1
    normed_own = normed.astype(BF16)
    normed_other = to_core(normed_own)
    up, down_t = outer_gather.placed(key, 0)
    activated, slope = column_call(
        up_kernel, "up", (normed_own, normed_other), up, (up_b[None],),
        ((2 * rows, BF16), (2 * rows, BF16)), 256,
    )
    ffn_other = to_core(product_back(activated[rows:], down_t, BF16))
    ffn = product_back(activated[:rows], down_t)
    second = normed + ffn + ffn_other.astype(F32) + down_b
    unit2, scale2 = normed_of(second)
    result = (unit2 * gain2 + bias2).astype(BF16)
    result = to_turned(result)
    result_pair = to_low(result)

    cot = own_grad.astype(F32) * row_valid
    final_gain_grad = jnp.sum(cot * unit2, axis=0)
    final_bias_grad = jnp.sum(cot, axis=0)
    d_second = norm_back(cot, gain2, unit2, scale2)
    d_ffn_own = d_second.astype(BF16)
    down_bias_grad = jnp.sum(d_ffn_own.astype(F32), axis=0)
    d_ffn_other = to_core(d_ffn_own)
    down_scatter = Scatter([(d_ffn_own, d_ffn_other, activated)], half)
    d_ffn = jnp.concatenate([d_ffn_own, after(d_ffn_other, *down_scatter.blocks)], axis=0)
    d_upper = (product(d_ffn, down_t) * slope.astype(F32)).astype(BF16)
    up_scatter = Scatter([(normed_own, normed_other, d_upper)], half, TAIL)
    d_upper = after(d_upper, *up_scatter.blocks)
    back_other = to_core(product_back(d_upper[rows:], up, BF16))
    sent = down_scatter.near(d_upper)
    back = product_back(after(d_upper, *sent)[:rows], up)
    d_normed = d_second + after(back, result, *down_scatter.early()) + back_other.astype(F32)
    norm_gain_grad = jnp.sum(d_normed * unit1, axis=0)
    norm_bias_grad = jnp.sum(d_normed, axis=0)
    d_first = norm_back(d_normed, gain1, unit1, scale1)
    d_attn_own = d_first.astype(BF16)
    out_bias_grad = jnp.sum(d_attn_own.astype(F32), axis=0)
    d_attn_other = to_core(d_attn_own)
    features = jnp.stack(
        [
            out_bias_grad,
            down_bias_grad,
            norm_gain_grad,
            norm_bias_grad,
            final_gain_grad,
            final_bias_grad,
        ]
    )
    extra = None
    if planes == 4:
        features = (features + to_core(features)).reshape(3, -1)
        extra = jnp.pad(features, ((1, TAIL - 4), (0, 4 * heads_width - features.shape[1])))
    d_attn = jnp.concatenate([d_attn_own, d_attn_other], axis=0)
    d_merged = product(d_attn, out_t, BF16)
    pairs = heads_width // PAIR
    part = pairs // 2
    back_args = (qkv, bias, merged, logs)
    d_qkv = attend_back(*back_args, d_merged, part, 0)
    down_pair = down_scatter.own(d_qkv)
    sent = up_scatter.near(*down_pair)
    d_merged = after(d_merged, d_qkv, result_pair, *sent)
    d_qkv = attend_back(*back_args, d_merged, pairs - part, part, (d_qkv,))
    down_part = down_scatter.part(d_qkv)
    down_high = to_high(down_part)
    inner_scatter = Scatter(
        [(own, other, after(d_qkv, down_part)), (d_attn_own, d_attn_other, merged)], half, TAIL, extra
    )
    pair = up_scatter.own(*inner_scatter.blocks)
    d_qkv = after(d_qkv, *pair)
    d_back = after(d_qkv, down_high, *inner_scatter.blocks)
    back_other = to_core(product_back(d_back[rows:], qkv_weight, BF16))
    back = product_back(d_back[:rows], qkv_weight)
    total = d_first + back + back_other.astype(F32)
    total = total.astype(BF16)
    up_part = up_scatter.part(back)
    up_high = to_high(up_part)
    inner_scatter.near(total, up_part)
    total = to_turned(total)
    pair = inner_scatter.own()
    total_pair = to_low(total)
    inner_part = inner_scatter.part(total_pair)
    result_pair = after(result_pair, *pair)
    layer_out = jnp.where(
        low == 0, jnp.stack([result, result_pair]), jnp.stack([result_pair, result])
    )
    input_grad = jnp.where(
        low == 0, jnp.stack([total, total_pair]), jnp.stack([total_pair, total])
    ).astype(F32)
    inner_high = to_high(inner_part)

    down_grad = summed(down_part, down_high).T
    up_sums = summed(up_part, up_high)
    up_grad = up_sums[:half]
    inner_sums = summed(inner_part, inner_high)
    query_grad, key_grad, value_grad = unweave(inner_sums[:half, :qkv_width])
    out_weight_grad = inner_sums[:half, qkv_width:].T
    if planes == 4:
        features = inner_sums[half + 1 : half + 4, : 2 * width].reshape(6, width)
        up_bias_grad = up_sums[half]
        query_bias_grad, _, value_bias_grad = (
            row[0] for row in unweave(inner_sums[half : half + 1, :qkv_width])
        )
    else:

        def spread(vector):
            empty = jnp.zeros_like(vector)
            return jnp.where(
                core == 0, jnp.concatenate([vector, empty]), jnp.concatenate([empty, vector])
            )

        sums = jnp.sum(d_qkv.astype(F32), axis=0, keepdims=True)
        query_sum, _, value_sum = (row[0] for row in unweave(sums))
        up_sum = jnp.sum(d_upper.astype(F32), axis=0)
        small = jnp.concatenate(
            [features.reshape(-1), spread(query_sum), spread(value_sum), spread(up_sum)]
        )
        small = lax.psum(small, AXES)
        features = small[: 6 * width].reshape(6, width)
        at = 6 * width

        def mine(start, size):
            return lax.dynamic_slice(small, (start + low * size,), (size,))

        query_bias_grad = mine(at, heads_width)
        value_bias_grad = mine(at + 2 * heads_width, heads_width)
        up_bias_grad = mine(at + 4 * heads_width, hidden)
    return (
        layer_out,
        input_grad,
        query_grad,
        key_grad,
        value_grad,
        out_weight_grad,
        up_grad,
        down_grad,
        query_bias_grad,
        value_bias_grad,
        features[0],
        up_bias_grad,
        features[1],
        features[2],
        features[3],
        features[4],
        features[5],
    )


def solution(mesh):
    in_specs = (
        P("fsdp", "ctx", None),
        P("fsdp"),
        P("fsdp", "ctx", None),
        P("fsdp", "tp"),
        P("fsdp", "tp"),
        P("fsdp", "tp"),
        P("tp", "fsdp"),
        P("fsdp", "tp"),
        P("tp", "fsdp"),
        P("tp"),
        P("tp"),
        P(),
        P("tp"),
        P(),
        P(),
        P(),
        P(),
        P(),
    )
    out_specs = (
        P("fsdp", "ctx", None),
        P("fsdp", "ctx", None),
        P("fsdp", "tp"),
        P("fsdp", "tp"),
        P("fsdp", "tp"),
        P("tp", "fsdp"),
        P("fsdp", "tp"),
        P("tp", "fsdp"),
        P("tp"),
        P("tp"),
        P(),
        P("tp"),
        P(),
        P(),
        P(),
        P(),
        P(),
    )
    return jax.shard_map(
        per_device, mesh=mesh, in_specs=in_specs, out_specs=out_specs, check_vma=False
    )
```

```python
import functools

import jax
import jax.numpy as jnp
from jax import lax
from jax.experimental import pallas as pl
from jax.experimental.pallas import tpu as pltpu
from jax.sharding import PartitionSpec as P

DH = 64
PAIR = 2 * DH
ROWS = 256

norm_eps = 1e-05
masked_score = -1e30
BF16 = jnp.bfloat16
F32 = jnp.float32
AXES = ("fsdp", "ctx", "tp")


def send(value, target):
    fsdp, ctx, tp = (lax.axis_size(axis) for axis in AXES)
    pairs = []
    kept = 0
    for f in range(fsdp):
        for h in range(ctx):
            for t in range(tp):
                plane, core, high, low = target(f // 2, f % 2, h, t)
                source = (f * ctx + h) * tp + t
                place_of = ((2 * plane + core) * ctx + high) * tp + low
                if source == place_of:
                    kept += 1
                else:
                    pairs.append((source, place_of))
    moved = lax.ppermute(value, AXES, pairs)
    if not kept:
        return moved
    plane, core = lax.axis_index("fsdp") // 2, lax.axis_index("fsdp") % 2
    high, low = lax.axis_index("ctx"), lax.axis_index("tp")
    _, at_core, at_high, at_low = target(plane, core, high, low)
    stays = (at_core == core) & (at_high == high) & (at_low == low)
    return jnp.where(stays, value, moved)


def to_core(value):
    return send(value, lambda p, c, h, t: (p, 1 - c, h, t))


def to_x(value):
    return send(value, lambda p, c, h, t: (p ^ 1, c, h, t))


def to_y(value):
    return send(value, lambda p, c, h, t: (p ^ 2, c, h, t))


def to_high(value):
    return send(value, lambda p, c, h, t: (p, c, 1 - h, t))


def to_low(value):
    return send(value, lambda p, c, h, t: (p, c, h, 1 - t))


def to_turned(value):
    return send(value, lambda p, c, h, t: (p, h, c, t))


def to_first(value):
    return send(value, lambda p, c, h, t: (p, t, h, c))


def to_second(value):
    return send(value, lambda p, c, h, t: (p, t, h, 1 - c))


def from_second(value):
    return send(value, lambda p, c, h, t: (p, 1 - t, h, c))


def plane_groups():
    fsdp = lax.axis_size("fsdp")
    return [[2 * p + c for p in range(fsdp // 2)] for c in range(2)]


def sorted_pair(first, second):
    low = lax.axis_index("tp")
    ahead = jnp.where(low == 0, first, second)
    behind = jnp.where(low == 0, second, first)
    return ahead, behind


def after(value, *others):
    return lax.optimization_barrier((value,) + others)[0]


def place_kernel(key_ref, *refs, homes, half, spans, outs):
    pieces = refs[: len(homes)]
    wholes, marks = refs[-1 - outs : -1], refs[-1]
    key = key_ref[0]
    copies = []
    for piece, blocks in zip(pieces, homes):
        for at, block in enumerate(blocks):
            start = pl.multiple_of((key ^ block) * half, half)
            for whole, (column, width) in zip(wholes, spans):
                copies.append(
                    pltpu.make_async_copy(
                        piece.at[pl.ds(at * half, half), pl.ds(column, width)],
                        whole.at[pl.ds(start, half), :],
                        marks.at[len(copies)],
                    )
                )
    for copy in copies:
        copy.start()
    for copy in copies:
        copy.wait()


def place(key, pieces, homes, half, spans, wholes=()):
    anywhere = pl.BlockSpec(memory_space=pl.ANY)
    near = pl.BlockSpec(memory_space=pltpu.VMEM)
    count = len(spans) * sum(len(home) for home in homes)
    first = 1 + len(pieces)
    return pl.pallas_call(
        functools.partial(place_kernel, homes=homes, half=half, spans=spans, outs=len(spans)),
        in_specs=[pl.BlockSpec(memory_space=pltpu.SMEM)]
        + [near] * len(pieces)
        + [anywhere] * len(wholes),
        out_specs=[anywhere] * len(spans),
        out_shape=[jax.ShapeDtypeStruct((8 * half, width), BF16) for _, width in spans],
        scratch_shapes=[pltpu.SemaphoreType.DMA((count,))],
        input_output_aliases={first + i: i for i in range(len(wholes))},
        name="place",
    )(key, *pieces, *wholes)


class Gather:
    def __init__(self, shard):
        self.half = shard.shape[0]
        self.width = shard.shape[1]
        self.first = to_first(shard)
        self.second = to_second(shard)
        self.planes = lax.axis_size("fsdp") // 2
        self.unit = jnp.concatenate([self.first, self.second], axis=0)

    def near(self, *others):
        if self.planes != 4:
            unit = jnp.concatenate(sorted_pair(self.first, self.second), axis=0)
            self.whole = lax.all_gather(
                unit, "fsdp", axis=0, tiled=True, axis_index_groups=plane_groups()
            )
            return
        self.unit = after(self.unit, *others)
        self.over_x = to_x(self.unit)
        self.over_y = to_y(self.unit)

    def far(self, spans):
        self.spans = spans
        self.sent = []
        self.cuts = ()
        for group in spans if self.planes == 4 else ():
            start, stop = group[0][0], group[-1][0] + group[-1][1]
            cut = lax.optimization_barrier(
                (self.over_x[: self.half, start:stop], self.over_y[self.half :, start:stop])
            )
            self.cuts += cut
            self.sent.append((start, to_y(cut[0]), to_x(cut[1])))

    def last(self):
        return self.sent[-1][1:] if self.planes == 4 else ()

    def placed(self, key, index):
        group = self.spans[index]
        if self.planes != 4:
            return [self.whole[:, a : a + n] for a, n in group]
        half = self.half
        pieces = (self.unit, self.over_x, self.over_y)
        homes = ((0, 1), (2, 3), (4, 5))
        start, first, second = self.sent[index]
        wholes = place(key, pieces, homes, half, group)
        moved = [(a - start, n) for a, n in group]
        return place(key, (first, second), ((6,), (7,)), half, moved, wholes)


TAIL = 16


def rows_kernel(at_ref, *refs, starts, half, tail, extra):
    count = len(starts) - 1
    lefts, rights = refs[: 2 * count], refs[2 * count : 3 * count]
    outs, turned = refs[3 * count + extra : -1], refs[-1]
    place_of = pl.program_id(0)
    tokens = turned.shape[1] // 2
    blocks = 8
    plane, low = at_ref[0], at_ref[1]
    if tail:

        @pl.when(place_of == 0)
        def _():
            row = lax.broadcasted_iota(jnp.int32, (tail, 2 * tokens), 0)
            turned[blocks * half :, :] = (row == 0).astype(F32).astype(BF16)

    for source in range(count):

        @pl.when(place_of == starts[source])
        def _(source=source):
            for block in range(blocks):
                step, side = block // 2, block % 2
                start = (2 * (plane ^ step) + (side ^ low)) * half
                start = pl.multiple_of(start, half)
                for part in range(2):
                    left = lefts[2 * source + part][:, pl.ds(start, half)]
                    turned[
                        block * half : (block + 1) * half, part * tokens : (part + 1) * tokens
                    ] = left.T

        @pl.when((place_of >= starts[source]) & (place_of < starts[source + 1]))
        def _(source=source):
            total = product(turned[...], rights[source][...])
            last = total[blocks * half :]
            if extra:
                last = last + refs[3 * count][...]
            total, last = total.astype(BF16), last.astype(BF16)
            for step, out in enumerate(outs[:3]):
                at = 2 * step * half
                out[:half, :] = total[at : at + half]
                if tail:
                    out[half : half + tail, :] = last
                out[half + tail :, :] = total[at + half : at + 2 * half]
            outs[3][:half, :] = total[6 * half : 7 * half]
            if tail:
                outs[3][half:, :] = last
            outs[4][...] = total[7 * half : 8 * half]


def row_blocks(at, sources, half, tail, extra):
    tile = 512
    starts = [0]
    for _, _, right in sources:
        starts.append(starts[-1] + right.shape[1] // tile)
    width = starts[-1] * tile
    tokens = sources[0][2].shape[0]
    features = sources[0][0].shape[1]
    outs = [2 * half + tail] * 3 + [half + tail, half]

    def right_spec(start, stop):
        return pl.BlockSpec(
            (tokens, tile), lambda i, at: (0, jnp.clip(i - start, 0, stop - start - 1))
        )

    operands, specs = [], []
    for own, other, _ in sources:
        operands += [own, other]
        specs += [pl.BlockSpec((tokens // 2, features), lambda i, at: (0, 0))] * 2
    for source, (_, _, right) in enumerate(sources):
        operands.append(right)
        specs.append(right_spec(starts[source], starts[source + 1]))
    if extra is not None:
        operands.append(extra)
        specs.append(pl.BlockSpec((tail, tile), lambda i, at: (0, i)))
    return pl.pallas_call(
        functools.partial(
            rows_kernel, starts=tuple(starts), half=half, tail=tail, extra=int(extra is not None)
        ),
        grid_spec=pltpu.PrefetchScalarGridSpec(
            num_scalar_prefetch=1,
            grid=(starts[-1],),
            in_specs=specs,
            out_specs=[pl.BlockSpec((rows, tile), lambda i, at: (0, i)) for rows in outs],
            scratch_shapes=[pltpu.VMEM((features + tail, tokens), BF16)],
        ),
        out_shape=[jax.ShapeDtypeStruct((rows, width), BF16) for rows in outs],
        cost_estimate=cheap(tokens * width),
        name="row_blocks",
    )(at, *operands)


def cheap(size):
    return pl.CostEstimate(flops=size, bytes_accessed=size // 4, transcendentals=0)


class Scatter:
    def __init__(self, sources, half, tail=0, extra=None):
        self.planes = lax.axis_size("fsdp") // 2
        self.half, self.tail = half, tail
        plane, low = lax.axis_index("fsdp") // 2, lax.axis_index("tp")
        if self.planes == 4:
            at = jnp.stack([plane, low]).astype(jnp.int32)
            self.blocks = row_blocks(at, sources, half, tail, extra)
            self.far_first = to_y(self.blocks[3])
            self.far_second = to_x(self.blocks[4])
        else:
            self.tail = 0
            whole = jnp.concatenate(
                [
                    row_product(jnp.concatenate([own, other], axis=0), right)
                    for own, other, right in sources
                ],
                axis=1,
            )
            mine = lax.psum_scatter(
                whole, "fsdp", scatter_dimension=0, tiled=True, axis_index_groups=plane_groups()
            )
            self.blocks = (jnp.concatenate(sorted_pair(mine[:half], mine[half:]), axis=0),)

    def tied(self, others):
        if others:
            return lax.optimization_barrier(tuple(self.blocks) + others)[: len(self.blocks)]
        return self.blocks

    def near(self, *others):
        if self.planes != 4:
            return ()
        half, tail = self.half, self.tail
        blocks = self.tied(others)
        over_x = added(blocks[1], jnp.pad(self.far_first, ((0, half), (0, 0))))
        over_y = added(blocks[2], jnp.pad(self.far_second, ((half + tail, 0), (0, 0))))
        sent = lax.optimization_barrier((over_x, over_y))
        self.over_x = to_x(sent[0])
        self.over_y = to_y(sent[1])
        return sent

    def arrivals(self):
        return (self.over_x, self.over_y) if self.planes == 4 else ()

    def own(self, *others):
        half, tail = self.half, self.tail
        total = self.tied(others)[0]
        if self.planes == 4:
            total = total.astype(F32) + self.over_x.astype(F32) + self.over_y.astype(F32)
        total = total.astype(BF16)
        pair = lax.optimization_barrier((total[: half + tail], total[half:]))
        self.landed = (to_first(pair[0]), from_second(pair[1]))
        return pair

    def part(self, *others):
        half, tail = self.half, self.tail
        first, second = after(self.landed[0], *others), self.landed[1]
        if tail:
            second = jnp.concatenate([second[tail:], second[:tail]], axis=0)
        return added(first, second)


def column_call(body, name, operands, weight, extras, outs, tile):
    width = weight.shape[1]

    def column_spec(rows):
        return pl.BlockSpec((rows, tile), lambda i: (0, i))

    return pl.pallas_call(
        body,
        grid=(width // tile,),
        in_specs=[pl.BlockSpec(left.shape, lambda i: (0, 0)) for left in operands]
        + [column_spec(array.shape[0]) for array in (weight,) + extras],
        out_specs=[column_spec(rows) for rows, _ in outs],
        out_shape=[jax.ShapeDtypeStruct((rows, width), kind) for rows, kind in outs],
        cost_estimate=cheap(weight.size),
        name=name,
    )(*operands, weight, *extras)


def up_kernel(own_ref, other_ref, weight_ref, bias_ref, active_ref, slope_ref):
    rows = own_ref.shape[0]
    for side, left in enumerate((own_ref, other_ref)):
        at = slice(side * rows, (side + 1) * rows)
        upper = product(left[...], weight_ref[...]) + bias_ref[...]
        cdf = 0.5 + 0.5 * lax.erf(upper * 0.5**0.5)
        active_ref[at, :] = (upper * cdf).astype(BF16)
        density = jnp.exp(upper * upper * -0.5) * (2 * jnp.pi) ** -0.5
        slope_ref[at, :] = (cdf + upper * density).astype(BF16)


def added(one, other):
    return (one.astype(F32) + other.astype(F32)).astype(BF16)


def summed(part, other):
    return part.astype(F32) + other.astype(F32)


def product(left, right, out=F32):
    return jnp.dot(left, right, preferred_element_type=F32).astype(out)


def product_back(left, right, out=F32):
    return lax.dot_general(
        left, right, (((1,), (1,)), ((), ())), preferred_element_type=F32
    ).astype(out)


def row_product(left, right, out=BF16):
    return lax.dot_general(
        left, right, (((0,), (0,)), ((), ())), preferred_element_type=F32
    ).astype(out)


def attend_kernel(qkv_ref, bias_ref, out_ref, log_ref):
    rows = qkv_ref.shape[0]
    low = lax.broadcasted_iota(jnp.int32, (1, PAIR), 1) < DH
    keys = qkv_ref[:, PAIR : 2 * PAIR]
    values = qkv_ref[:, 2 * PAIR :]
    bias = bias_ref[...]
    zero = jnp.zeros((), BF16)
    picks = (low, jnp.logical_not(low))
    head_values = [jnp.where(pick, values, zero) for pick in picks]
    for tile in range(rows // ROWS):
        at = slice(tile * ROWS, (tile + 1) * ROWS)
        query = qkv_ref[at, :PAIR]
        out = jnp.zeros((ROWS, PAIR), F32)
        logs = jnp.zeros((ROWS, PAIR), F32)
        for head in range(2):
            mine = jnp.where(picks[head], query, zero)
            scores = product_back(mine, keys) + bias
            top = jnp.max(scores, axis=1, keepdims=True)
            weights = jnp.exp(scores - top)
            total = jnp.sum(weights, axis=1, keepdims=True)
            out = out + product(weights.astype(BF16), head_values[head]) / total
            logs = jnp.where(picks[head], top + jnp.log(total), logs)
        out_ref[at, :] = out.astype(BF16)
        log_ref[at, :] = logs


def attend(qkv, bias):
    rows = qkv.shape[0]
    pairs = qkv.shape[1] // (3 * PAIR)
    flops = 2 * 2 * 2 * pairs * rows * rows * DH
    return pl.pallas_call(
        attend_kernel,
        grid=(pairs,),
        in_specs=[
            pl.BlockSpec((rows, 3 * PAIR), lambda i: (0, i)),
            pl.BlockSpec((1, rows), lambda i: (0, 0)),
        ],
        out_specs=[
            pl.BlockSpec((rows, PAIR), lambda i: (0, i)),
            pl.BlockSpec((rows, PAIR), lambda i: (0, i)),
        ],
        out_shape=[
            jax.ShapeDtypeStruct((rows, pairs * PAIR), BF16),
            jax.ShapeDtypeStruct((rows, pairs * PAIR), F32),
        ],
        cost_estimate=pl.CostEstimate(
            flops=flops // 64, bytes_accessed=rows * pairs * PAIR, transcendentals=0,
        ),
        name="attend",
    )(qkv, bias)


def attend_back_kernel(
    qkv_ref, bias_ref, out_ref, log_ref, grad_ref, result_ref, key_acc, value_acc
):
    rows = qkv_ref.shape[0]
    low = lax.broadcasted_iota(jnp.int32, (1, PAIR), 1) < DH
    keys = qkv_ref[:, PAIR : 2 * PAIR]
    values = qkv_ref[:, 2 * PAIR :]
    bias = bias_ref[...]
    zero = jnp.zeros((), BF16)
    picks = (low, jnp.logical_not(low))
    head_keys = [jnp.where(pick, keys, zero) for pick in picks]
    for tile in range(rows // ROWS):
        at = slice(tile * ROWS, (tile + 1) * ROWS)
        query = qkv_ref[at, :PAIR]
        grad = grad_ref[at, :]
        both = grad.astype(F32) * out_ref[at, :].astype(F32)
        query_grad = jnp.zeros((ROWS, PAIR), F32)
        key_grad = jnp.zeros((rows, PAIR), F32)
        value_grad = jnp.zeros((rows, PAIR), F32)
        for head in range(2):
            pick = picks[head]
            mine = jnp.where(pick, query, zero)
            mine_grad = jnp.where(pick, grad, zero)
            delta = jnp.sum(jnp.where(pick, both, 0.0), axis=1, keepdims=True)
            logs = log_ref[at, head * DH : head * DH + 1]
            prob = jnp.exp(product_back(mine, keys) + bias - logs)
            d_prob = product_back(mine_grad, values)
            d_scores = (prob * (d_prob - delta)).astype(BF16)
            query_grad = query_grad + product(d_scores, head_keys[head])
            key_grad = key_grad + row_product(d_scores, mine, F32)
            value_grad = value_grad + row_product(prob.astype(BF16), mine_grad, F32)
        query_grad = query_grad * DH**-0.5
        result_ref[at, :PAIR] = query_grad.astype(BF16)
        if tile == 0:
            key_acc[...] = key_grad
            value_acc[...] = value_grad
        else:
            key_acc[...] += key_grad
            value_acc[...] += value_grad
    result_ref[:, PAIR : 2 * PAIR] = key_acc[...].astype(BF16)
    result_ref[:, 2 * PAIR :] = value_acc[...].astype(BF16)


def attend_back(qkv, bias, out, logs, grad, pairs, begin, into=()):
    rows = qkv.shape[0]
    wide = pl.BlockSpec((rows, 3 * PAIR), lambda i: (0, i + begin))
    narrow = pl.BlockSpec((rows, PAIR), lambda i: (0, i + begin))

    def kernel(*refs):
        attend_back_kernel(*refs[:5], *refs[5 + len(into) :])

    return pl.pallas_call(
        kernel,
        grid=(pairs,),
        in_specs=[wide, pl.BlockSpec((1, rows), lambda i: (0, 0)), narrow, narrow, narrow]
        + [pl.BlockSpec(memory_space=pl.ANY)] * len(into),
        out_specs=wide,
        out_shape=jax.ShapeDtypeStruct(qkv.shape, BF16),
        scratch_shapes=[pltpu.VMEM((rows, PAIR), F32)] * 2,
        input_output_aliases={5: 0} if into else {},
        cost_estimate=cheap(rows * rows),
        name="attend_back",
    )(qkv, bias, out, logs, grad, *into)


def normed_of(hidden):
    centred = hidden - jnp.mean(hidden, axis=-1, keepdims=True)
    spread = jnp.mean(centred * centred, axis=-1, keepdims=True)
    scale = lax.rsqrt(spread + norm_eps)
    return centred * scale, scale


def norm_back(grad, gain, unit, scale):
    inner = grad * gain
    return scale * (
        inner
        - jnp.mean(inner, axis=-1, keepdims=True)
        - unit * jnp.mean(inner * unit, axis=-1, keepdims=True)
    )


def finish_kernel(part_ref, high_ref, query_ref, key_ref, value_ref, out_ref, tail_ref, *, half):
    total = part_ref[...].astype(F32) + high_ref[...].astype(F32)
    width = query_ref.shape[1]
    for pair in range(width // PAIR):
        at = slice(pair * PAIR, (pair + 1) * PAIR)
        for place_of, ref in enumerate((query_ref, key_ref, value_ref)):
            start = (3 * pair + place_of) * PAIR
            ref[:, at] = total[:half, start : start + PAIR]
    out_ref[...] = total[:half, 3 * width :].T
    tail_ref[...] = total[half:]


def finish(part, high, half, width):
    columns = part.shape[1]
    tail = part.shape[0] - half
    return pl.pallas_call(
        functools.partial(finish_kernel, half=half),
        out_shape=[jax.ShapeDtypeStruct((half, width), F32)] * 3
        + [
            jax.ShapeDtypeStruct((columns - 3 * width, half), F32),
            jax.ShapeDtypeStruct((tail, columns), F32),
        ],
        cost_estimate=cheap(part.size),
        name="finish",
    )(part, high)


def weave(parts):
    lead = parts[0].shape[0]
    parts = [part.reshape(lead, -1, PAIR) for part in parts]
    return jnp.stack(parts, axis=2).reshape(lead, -1)


def unweave(woven):
    lead = woven.shape[0]
    woven = woven.reshape(lead, -1, 3, PAIR)
    return [woven[:, :, part].reshape(lead, -1) for part in range(3)]


def per_device(
    layer_in,
    lengths,
    out_grad,
    query_weight,
    key_weight,
    value_weight,
    out_weight,
    up_weight,
    down_weight,
    query_bias,
    value_bias,
    out_bias,
    up_bias,
    down_bias,
    norm_gain,
    norm_bias,
    final_gain,
    final_bias,
):
    fsdp = lax.axis_index("fsdp")
    plane, core = fsdp // 2, fsdp % 2
    high, low = lax.axis_index("ctx"), lax.axis_index("tp")
    planes = lax.axis_size("fsdp") // 2
    half = query_weight.shape[0]
    rows = layer_in.shape[1]
    width = layer_in.shape[2]
    heads_width = query_weight.shape[1]
    hidden = up_weight.shape[1]
    key = (2 * plane + low).astype(jnp.int32)[None]
    qkv_width = 3 * heads_width
    inner_gather = Gather(
        jnp.concatenate([weave([query_weight, key_weight, value_weight]), out_weight.T], axis=1)
    )
    mine_in = lax.dynamic_index_in_dim(layer_in, low, 0, keepdims=False)
    own = to_turned(mine_in)
    length = lax.dynamic_index_in_dim(to_turned(lengths), low, 0, keepdims=False)
    inner_gather.near()
    outer_shard = jnp.concatenate([up_weight, down_weight.T], axis=1)
    outer_gather = Gather(after(outer_shard, inner_gather.first, inner_gather.second))
    inner_gather.far((((0, qkv_width), (qkv_width, heads_width)),))
    arrived = inner_gather.last()
    other = to_core(own)
    vectors = to_first(after(jnp.concatenate([query_bias, value_bias, up_bias]), own, *arrived))
    if planes == 4:
        outer_gather.near(inner_gather.over_x, inner_gather.over_y, other)
    else:
        outer_gather.near()
    mine_grad = lax.dynamic_index_in_dim(out_grad, low, 0, keepdims=False)
    own_grad = to_turned(after(mine_grad, own))
    qkv_weight, out_t = inner_gather.placed(key, 0)
    own = after(own, outer_gather.unit)

    out_b, down_b, gain1, bias1, gain2, bias2 = (
        out_bias, down_bias, norm_gain, norm_bias, final_gain, final_bias
    )
    query_b = vectors[:heads_width]
    value_b = vectors[heads_width : 2 * heads_width]
    up_b = vectors[2 * heads_width :]
    qkv_b = weave([query_b[None], jnp.zeros_like(query_b)[None], value_b[None]])
    scales = weave(
        [
            jnp.full((1, heads_width), DH**-0.5, F32),
            jnp.ones((1, heads_width), F32),
            jnp.ones((1, heads_width), F32),
        ]
    )
    places = lax.iota(jnp.int32, rows)
    own_places = core * rows + places
    other_places = (1 - core) * rows + places
    valid = jnp.concatenate([own_places, other_places]) < length
    bias = jnp.where(valid, 0.0, masked_score).astype(F32)[None, :]
    row_valid = (own_places < length).astype(F32)[:, None]

    x = jnp.concatenate([own, other], axis=0)
    qkv = ((product(x, qkv_weight) + qkv_b) * scales).astype(BF16)
    merged, logs = attend(qkv, bias)
    if planes == 4:
        merged = after(merged, own_grad)
    outer_gather.far((((0, hidden), (hidden, hidden)),))
    attn_other = to_core(product_back(merged[rows:], out_t, BF16))
    attn = product_back(merged[:rows], out_t)
    first = own.astype(F32) + attn + attn_other.astype(F32) + out_b
    unit1, scale1 = normed_of(first)
    normed = unit1 * gain1 + bias1
    normed_own = normed.astype(BF16)
    normed_other = to_core(normed_own)
    up, down_t = outer_gather.placed(key, 0)
    activated, slope = column_call(
        up_kernel, "up", (normed_own, normed_other), up, (up_b[None],),
        ((2 * rows, BF16), (2 * rows, BF16)), 256,
    )
    ffn_other = to_core(product_back(activated[rows:], down_t, BF16))
    ffn = product_back(activated[:rows], down_t)
    second = normed + ffn + ffn_other.astype(F32) + down_b
    unit2, scale2 = normed_of(second)
    result = (unit2 * gain2 + bias2).astype(BF16)
    result = to_turned(result)
    result_pair = to_low(result)

    cot = own_grad.astype(F32) * row_valid
    final_gain_grad = jnp.sum(cot * unit2, axis=0)
    final_bias_grad = jnp.sum(cot, axis=0)
    d_second = norm_back(cot, gain2, unit2, scale2)
    d_ffn_own = d_second.astype(BF16)
    down_bias_grad = jnp.sum(d_ffn_own.astype(F32), axis=0)
    d_ffn_other = to_core(d_ffn_own)
    down_scatter = Scatter([(d_ffn_own, d_ffn_other, activated)], half)
    d_ffn = jnp.concatenate([d_ffn_own, after(d_ffn_other, *down_scatter.blocks)], axis=0)
    d_upper = (product(d_ffn, down_t) * slope.astype(F32)).astype(BF16)
    up_bias_grad = jnp.sum(d_upper.astype(F32), axis=0)
    sent = down_scatter.near(d_upper)
    up_scatter = Scatter([(normed_own, normed_other, after(d_upper, *sent))], half)
    d_upper = after(d_upper, *up_scatter.blocks)
    back_other = to_core(product_back(d_upper[rows:], up, BF16))
    back = product_back(d_upper[:rows], up)
    d_normed = d_second + after(back, result, *down_scatter.arrivals()) + back_other.astype(F32)
    norm_gain_grad = jnp.sum(d_normed * unit1, axis=0)
    norm_bias_grad = jnp.sum(d_normed, axis=0)
    d_first = norm_back(d_normed, gain1, unit1, scale1)
    d_attn_own = d_first.astype(BF16)
    out_bias_grad = jnp.sum(d_attn_own.astype(F32), axis=0)
    d_attn_other = to_core(d_attn_own)
    features = jnp.stack(
        [
            out_bias_grad,
            down_bias_grad,
            norm_gain_grad,
            norm_bias_grad,
            final_gain_grad,
            final_bias_grad,
        ]
    )
    extra = None
    if planes == 4:
        features = (features + to_core(features)).reshape(3, -1)
        extra = jnp.concatenate([features, up_bias_grad[None]], axis=0)
        extra = jnp.pad(extra, ((1, TAIL - 5), (0, 0)))
    d_attn = jnp.concatenate([d_attn_own, d_attn_other], axis=0)
    d_merged = product(d_attn, out_t, BF16)
    down_pair = down_scatter.own()
    pairs = heads_width // PAIR
    part = pairs // 2
    back_args = (qkv, bias, merged, logs)
    d_merged = after(d_merged, *down_pair)
    d_qkv = attend_back(*back_args, d_merged, part, 0)
    sent = up_scatter.near(d_qkv)
    down_part = down_scatter.part(d_qkv)
    down_high = to_high(down_part)
    d_merged = after(d_merged, d_qkv, result_pair, down_part, *sent)
    d_qkv = attend_back(*back_args, d_merged, pairs - part, part, (d_qkv,))
    inner_scatter = Scatter(
        [(own, other, d_qkv), (d_attn_own, d_attn_other, merged)], half, TAIL, extra
    )
    pair = up_scatter.own(*inner_scatter.blocks)
    d_qkv = after(d_qkv, *pair)
    d_back = after(d_qkv, down_high, *inner_scatter.blocks)
    back_other = to_core(product_back(d_back[rows:], qkv_weight, BF16))
    back = product_back(d_back[:rows], qkv_weight)
    total = d_first + back + back_other.astype(F32)
    total = total.astype(BF16)
    up_part = up_scatter.part(back)
    up_high = to_high(up_part)
    inner_scatter.near(total, up_part)
    total = to_turned(total)
    pair = inner_scatter.own()
    total_pair = to_low(total)
    inner_part = inner_scatter.part(up_high)
    result_pair = after(result_pair, *pair)
    layer_out = jnp.where(
        low == 0, jnp.stack([result, result_pair]), jnp.stack([result_pair, result])
    )
    input_grad = jnp.where(
        low == 0, jnp.stack([total, total_pair]), jnp.stack([total_pair, total])
    ).astype(F32)
    inner_high = to_high(inner_part)

    down_grad = summed(down_part, down_high).T
    up_sums = summed(up_part, up_high)
    up_grad = up_sums[:half]
    inner_high = after(inner_high, total_pair)
    if planes == 4:
        query_grad, key_grad, value_grad, out_weight_grad, tail = finish(
            inner_part, inner_high, half, heads_width
        )
        features = tail[1:4, : 2 * width].reshape(6, width)
        up_bias_grad = tail[4]
        query_bias_grad, _, value_bias_grad = (row[0] for row in unweave(tail[:1, :qkv_width]))
    else:
        inner_sums = summed(inner_part, inner_high)
        query_grad, key_grad, value_grad = unweave(inner_sums[:half, :qkv_width])
        out_weight_grad = inner_sums[:half, qkv_width:].T

        def spread(vector):
            empty = jnp.zeros_like(vector)
            return jnp.where(
                core == 0, jnp.concatenate([vector, empty]), jnp.concatenate([empty, vector])
            )

        sums = jnp.sum(d_qkv.astype(F32), axis=0, keepdims=True)
        query_sum, _, value_sum = (row[0] for row in unweave(sums))
        up_sum = up_bias_grad
        small = jnp.concatenate(
            [features.reshape(-1), spread(query_sum), spread(value_sum), spread(up_sum)]
        )
        small = lax.psum(small, AXES)
        features = small[: 6 * width].reshape(6, width)
        at = 6 * width

        def mine(start, size):
            return lax.dynamic_slice(small, (start + low * size,), (size,))

        query_bias_grad = mine(at, heads_width)
        value_bias_grad = mine(at + 2 * heads_width, heads_width)
        up_bias_grad = mine(at + 4 * heads_width, hidden)
    return (
        layer_out,
        input_grad,
        query_grad,
        key_grad,
        value_grad,
        out_weight_grad,
        up_grad,
        down_grad,
        query_bias_grad,
        value_bias_grad,
        features[0],
        up_bias_grad,
        features[1],
        features[2],
        features[3],
        features[4],
        features[5],
    )


def solution(mesh):
    in_specs = (
        P("fsdp", "ctx", None),
        P("fsdp"),
        P("fsdp", "ctx", None),
        P("fsdp", "tp"),
        P("fsdp", "tp"),
        P("fsdp", "tp"),
        P("tp", "fsdp"),
        P("fsdp", "tp"),
        P("tp", "fsdp"),
        P("tp"),
        P("tp"),
        P(),
        P("tp"),
        P(),
        P(),
        P(),
        P(),
        P(),
    )
    out_specs = (
        P("fsdp", "ctx", None),
        P("fsdp", "ctx", None),
        P("fsdp", "tp"),
        P("fsdp", "tp"),
        P("fsdp", "tp"),
        P("tp", "fsdp"),
        P("fsdp", "tp"),
        P("tp", "fsdp"),
        P("tp"),
        P("tp"),
        P(),
        P("tp"),
        P(),
        P(),
        P(),
        P(),
        P(),
    )
    return jax.shard_map(
        per_device, mesh=mesh, in_specs=in_specs, out_specs=out_specs, check_vma=False
    )
```

```python
import functools

import jax
import jax.numpy as jnp
from jax import lax
from jax.experimental import pallas as pl
from jax.experimental.pallas import tpu as pltpu
from jax.sharding import PartitionSpec as P

DH = 64
PAIR = 2 * DH
ROWS = 256

norm_eps = 1e-05
masked_score = -1e30
BF16 = jnp.bfloat16
F32 = jnp.float32
AXES = ("fsdp", "ctx", "tp")


def send(value, target):
    fsdp, ctx, tp = (lax.axis_size(axis) for axis in AXES)
    pairs = []
    kept = 0
    for f in range(fsdp):
        for h in range(ctx):
            for t in range(tp):
                plane, core, high, low = target(f // 2, f % 2, h, t)
                source = (f * ctx + h) * tp + t
                place_of = ((2 * plane + core) * ctx + high) * tp + low
                if source == place_of:
                    kept += 1
                else:
                    pairs.append((source, place_of))
    moved = lax.ppermute(value, AXES, pairs)
    if not kept:
        return moved
    plane, core = lax.axis_index("fsdp") // 2, lax.axis_index("fsdp") % 2
    high, low = lax.axis_index("ctx"), lax.axis_index("tp")
    _, at_core, at_high, at_low = target(plane, core, high, low)
    stays = (at_core == core) & (at_high == high) & (at_low == low)
    return jnp.where(stays, value, moved)


def to_core(value):
    return send(value, lambda p, c, h, t: (p, 1 - c, h, t))


def to_x(value):
    return send(value, lambda p, c, h, t: (p ^ 1, c, h, t))


def to_y(value):
    return send(value, lambda p, c, h, t: (p ^ 2, c, h, t))


def to_high(value):
    return send(value, lambda p, c, h, t: (p, c, 1 - h, t))


def to_low(value):
    return send(value, lambda p, c, h, t: (p, c, h, 1 - t))


def to_turned(value):
    return send(value, lambda p, c, h, t: (p, h, c, t))


def to_first(value):
    return send(value, lambda p, c, h, t: (p, t, h, c))


def to_second(value):
    return send(value, lambda p, c, h, t: (p, t, h, 1 - c))


def from_second(value):
    return send(value, lambda p, c, h, t: (p, 1 - t, h, c))


def plane_groups():
    fsdp = lax.axis_size("fsdp")
    return [[2 * p + c for p in range(fsdp // 2)] for c in range(2)]


def sorted_pair(first, second):
    low = lax.axis_index("tp")
    ahead = jnp.where(low == 0, first, second)
    behind = jnp.where(low == 0, second, first)
    return ahead, behind


def after(value, *others):
    return lax.optimization_barrier((value,) + others)[0]


def place_kernel(key_ref, *refs, homes, half, spans, outs):
    pieces = refs[: len(homes)]
    wholes, marks = refs[-1 - outs : -1], refs[-1]
    key = key_ref[0]
    copies = []
    for piece, blocks in zip(pieces, homes):
        for at, block in enumerate(blocks):
            start = pl.multiple_of((key ^ block) * half, half)
            for whole, (column, width) in zip(wholes, spans):
                copies.append(
                    pltpu.make_async_copy(
                        piece.at[pl.ds(at * half, half), pl.ds(column, width)],
                        whole.at[pl.ds(start, half), :],
                        marks.at[len(copies)],
                    )
                )
    for copy in copies:
        copy.start()
    for copy in copies:
        copy.wait()


def place(key, pieces, homes, half, spans, wholes=()):
    anywhere = pl.BlockSpec(memory_space=pl.ANY)
    near = pl.BlockSpec(memory_space=pltpu.VMEM)
    count = len(spans) * sum(len(home) for home in homes)
    first = 1 + len(pieces)
    return pl.pallas_call(
        functools.partial(place_kernel, homes=homes, half=half, spans=spans, outs=len(spans)),
        in_specs=[pl.BlockSpec(memory_space=pltpu.SMEM)]
        + [near] * len(pieces)
        + [anywhere] * len(wholes),
        out_specs=[anywhere] * len(spans),
        out_shape=[jax.ShapeDtypeStruct((8 * half, width), BF16) for _, width in spans],
        scratch_shapes=[pltpu.SemaphoreType.DMA((count,))],
        input_output_aliases={first + i: i for i in range(len(wholes))},
        name="place",
    )(key, *pieces, *wholes)


class Gather:
    def __init__(self, shard):
        self.half = shard.shape[0]
        self.width = shard.shape[1]
        self.first = to_first(shard)
        self.second = to_second(shard)
        self.planes = lax.axis_size("fsdp") // 2
        self.unit = jnp.concatenate([self.first, self.second], axis=0)

    def near(self, *others):
        if self.planes != 4:
            unit = jnp.concatenate(sorted_pair(self.first, self.second), axis=0)
            self.whole = lax.all_gather(
                unit, "fsdp", axis=0, tiled=True, axis_index_groups=plane_groups()
            )
            return
        self.unit = after(self.unit, *others)
        self.over_x = to_x(self.unit)
        self.over_y = to_y(self.unit)

    def far(self, spans):
        self.spans = spans
        self.sent = []
        self.cuts = ()
        for group in spans if self.planes == 4 else ():
            start, stop = group[0][0], group[-1][0] + group[-1][1]
            cut = lax.optimization_barrier(
                (self.over_x[: self.half, start:stop], self.over_y[self.half :, start:stop])
            )
            self.cuts += cut
            self.sent.append((start, to_y(cut[0]), to_x(cut[1])))

    def last(self):
        return self.sent[-1][1:] if self.planes == 4 else ()

    def placed(self, key, index):
        group = self.spans[index]
        if self.planes != 4:
            return [self.whole[:, a : a + n] for a, n in group]
        half = self.half
        pieces = (self.unit, self.over_x, self.over_y)
        homes = ((0, 1), (2, 3), (4, 5))
        start, first, second = self.sent[index]
        wholes = place(key, pieces, homes, half, group)
        moved = [(a - start, n) for a, n in group]
        return place(key, (first, second), ((6,), (7,)), half, moved, wholes)


TAIL = 16


def rows_kernel(at_ref, *refs, starts, half, tail, extra):
    count = len(starts) - 1
    lefts, rights = refs[: 2 * count], refs[2 * count : 3 * count]
    outs, turned = refs[3 * count + extra : -1], refs[-1]
    place_of = pl.program_id(0)
    tokens = turned.shape[1] // 2
    blocks = 8
    plane, low = at_ref[0], at_ref[1]
    if tail:

        @pl.when(place_of == 0)
        def _():
            row = lax.broadcasted_iota(jnp.int32, (tail, 2 * tokens), 0)
            turned[blocks * half :, :] = (row == 0).astype(F32).astype(BF16)

    for source in range(count):

        @pl.when(place_of == starts[source])
        def _(source=source):
            for block in range(blocks):
                step, side = block // 2, block % 2
                start = (2 * (plane ^ step) + (side ^ low)) * half
                start = pl.multiple_of(start, half)
                for part in range(2):
                    left = lefts[2 * source + part][:, pl.ds(start, half)]
                    turned[
                        block * half : (block + 1) * half, part * tokens : (part + 1) * tokens
                    ] = left.T

        @pl.when((place_of >= starts[source]) & (place_of < starts[source + 1]))
        def _(source=source):
            total = product(turned[...], rights[source][...])
            last = total[blocks * half :]
            if extra:
                last = last + refs[3 * count][...]
            total, last = total.astype(BF16), last.astype(BF16)
            for step, out in enumerate(outs[:3]):
                at = 2 * step * half
                out[:half, :] = total[at : at + half]
                if tail:
                    out[half : half + tail, :] = last
                out[half + tail :, :] = total[at + half : at + 2 * half]
            outs[3][:half, :] = total[6 * half : 7 * half]
            if tail:
                outs[3][half:, :] = last
            outs[4][...] = total[7 * half : 8 * half]


def row_blocks(at, sources, half, tail, extra):
    tile = 512
    starts = [0]
    for _, _, right in sources:
        starts.append(starts[-1] + right.shape[1] // tile)
    width = starts[-1] * tile
    tokens = sources[0][2].shape[0]
    features = sources[0][0].shape[1]
    outs = [2 * half + tail] * 3 + [half + tail, half]

    def right_spec(start, stop):
        return pl.BlockSpec(
            (tokens, tile), lambda i, at: (0, jnp.clip(i - start, 0, stop - start - 1))
        )

    operands, specs = [], []
    for own, other, _ in sources:
        operands += [own, other]
        specs += [pl.BlockSpec((tokens // 2, features), lambda i, at: (0, 0))] * 2
    for source, (_, _, right) in enumerate(sources):
        operands.append(right)
        specs.append(right_spec(starts[source], starts[source + 1]))
    if extra is not None:
        operands.append(extra)
        specs.append(pl.BlockSpec((tail, tile), lambda i, at: (0, i)))
    return pl.pallas_call(
        functools.partial(
            rows_kernel, starts=tuple(starts), half=half, tail=tail, extra=int(extra is not None)
        ),
        grid_spec=pltpu.PrefetchScalarGridSpec(
            num_scalar_prefetch=1,
            grid=(starts[-1],),
            in_specs=specs,
            out_specs=[pl.BlockSpec((rows, tile), lambda i, at: (0, i)) for rows in outs],
            scratch_shapes=[pltpu.VMEM((features + tail, tokens), BF16)],
        ),
        out_shape=[jax.ShapeDtypeStruct((rows, width), BF16) for rows in outs],
        cost_estimate=cheap(tokens * width),
        name="row_blocks",
    )(at, *operands)


def cheap(size):
    return pl.CostEstimate(flops=size, bytes_accessed=size // 4, transcendentals=0)


class Scatter:
    def __init__(self, sources, half, tail=0, extra=None):
        self.planes = lax.axis_size("fsdp") // 2
        self.half, self.tail = half, tail
        plane, low = lax.axis_index("fsdp") // 2, lax.axis_index("tp")
        if self.planes == 4:
            at = jnp.stack([plane, low]).astype(jnp.int32)
            self.blocks = row_blocks(at, sources, half, tail, extra)
            self.far_first = to_y(self.blocks[3])
            self.far_second = to_x(self.blocks[4])
        else:
            self.tail = 0
            whole = jnp.concatenate(
                [
                    row_product(jnp.concatenate([own, other], axis=0), right)
                    for own, other, right in sources
                ],
                axis=1,
            )
            mine = lax.psum_scatter(
                whole, "fsdp", scatter_dimension=0, tiled=True, axis_index_groups=plane_groups()
            )
            self.blocks = (jnp.concatenate(sorted_pair(mine[:half], mine[half:]), axis=0),)

    def tied(self, others):
        if others:
            return lax.optimization_barrier(tuple(self.blocks) + others)[: len(self.blocks)]
        return self.blocks

    def near(self, *others):
        if self.planes != 4:
            return ()
        half, tail = self.half, self.tail
        blocks = self.tied(others)
        over_x = added(blocks[1], jnp.pad(self.far_first, ((0, half), (0, 0))))
        over_y = added(blocks[2], jnp.pad(self.far_second, ((half + tail, 0), (0, 0))))
        sent = lax.optimization_barrier((over_x, over_y))
        self.over_x = to_x(sent[0])
        self.over_y = to_y(sent[1])
        return sent

    def arrivals(self):
        return (self.over_x, self.over_y) if self.planes == 4 else ()

    def own(self, *others):
        half, tail = self.half, self.tail
        total = self.tied(others)[0]
        if self.planes == 4:
            total = total.astype(F32) + self.over_x.astype(F32) + self.over_y.astype(F32)
        total = total.astype(BF16)
        pair = lax.optimization_barrier((total[: half + tail], total[half:]))
        self.landed = (to_first(pair[0]), from_second(pair[1]))
        return pair

    def part(self, *others):
        half, tail = self.half, self.tail
        first, second = after(self.landed[0], *others), self.landed[1]
        if tail:
            second = jnp.concatenate([second[tail:], second[:tail]], axis=0)
        return added(first, second)


def column_call(body, name, operands, weight, extras, outs, tile):
    width = weight.shape[1]

    def column_spec(rows):
        return pl.BlockSpec((rows, tile), lambda i: (0, i))

    return pl.pallas_call(
        body,
        grid=(width // tile,),
        in_specs=[pl.BlockSpec(left.shape, lambda i: (0, 0)) for left in operands]
        + [column_spec(array.shape[0]) for array in (weight,) + extras],
        out_specs=[column_spec(rows) for rows, _ in outs],
        out_shape=[jax.ShapeDtypeStruct((rows, width), kind) for rows, kind in outs],
        cost_estimate=cheap(weight.size),
        name=name,
    )(*operands, weight, *extras)


def up_kernel(own_ref, other_ref, weight_ref, bias_ref, active_ref, slope_ref):
    rows = own_ref.shape[0]
    for side, left in enumerate((own_ref, other_ref)):
        at = slice(side * rows, (side + 1) * rows)
        upper = product(left[...], weight_ref[...]) + bias_ref[...]
        cdf = 0.5 + 0.5 * lax.erf(upper * 0.5**0.5)
        active_ref[at, :] = (upper * cdf).astype(BF16)
        density = jnp.exp(upper * upper * -0.5) * (2 * jnp.pi) ** -0.5
        slope_ref[at, :] = (cdf + upper * density).astype(BF16)


def added(one, other):
    return (one.astype(F32) + other.astype(F32)).astype(BF16)


def summed(part, other):
    return part.astype(F32) + other.astype(F32)


def product(left, right, out=F32):
    return jnp.dot(left, right, preferred_element_type=F32).astype(out)


def product_back(left, right, out=F32):
    return lax.dot_general(
        left, right, (((1,), (1,)), ((), ())), preferred_element_type=F32
    ).astype(out)


def row_product(left, right, out=BF16):
    return lax.dot_general(
        left, right, (((0,), (0,)), ((), ())), preferred_element_type=F32
    ).astype(out)


def attend_kernel(qkv_ref, bias_ref, out_ref, log_ref):
    rows = qkv_ref.shape[0]
    low = lax.broadcasted_iota(jnp.int32, (1, PAIR), 1) < DH
    keys = qkv_ref[:, PAIR : 2 * PAIR]
    values = qkv_ref[:, 2 * PAIR :]
    bias = bias_ref[...]
    zero = jnp.zeros((), BF16)
    picks = (low, jnp.logical_not(low))
    head_values = [jnp.where(pick, values, zero) for pick in picks]
    for tile in range(rows // ROWS):
        at = slice(tile * ROWS, (tile + 1) * ROWS)
        query = qkv_ref[at, :PAIR]
        out = jnp.zeros((ROWS, PAIR), F32)
        logs = jnp.zeros((ROWS, PAIR), F32)
        for head in range(2):
            mine = jnp.where(picks[head], query, zero)
            scores = product_back(mine, keys) + bias
            top = jnp.max(scores, axis=1, keepdims=True)
            weights = jnp.exp(scores - top)
            total = jnp.sum(weights, axis=1, keepdims=True)
            out = out + product(weights.astype(BF16), head_values[head]) / total
            logs = jnp.where(picks[head], top + jnp.log(total), logs)
        out_ref[at, :] = out.astype(BF16)
        log_ref[at, :] = logs


def attend(qkv, bias):
    rows = qkv.shape[0]
    pairs = qkv.shape[1] // (3 * PAIR)
    flops = 2 * 2 * 2 * pairs * rows * rows * DH
    return pl.pallas_call(
        attend_kernel,
        grid=(pairs,),
        in_specs=[
            pl.BlockSpec((rows, 3 * PAIR), lambda i: (0, i)),
            pl.BlockSpec((1, rows), lambda i: (0, 0)),
        ],
        out_specs=[
            pl.BlockSpec((rows, PAIR), lambda i: (0, i)),
            pl.BlockSpec((rows, PAIR), lambda i: (0, i)),
        ],
        out_shape=[
            jax.ShapeDtypeStruct((rows, pairs * PAIR), BF16),
            jax.ShapeDtypeStruct((rows, pairs * PAIR), F32),
        ],
        cost_estimate=pl.CostEstimate(
            flops=flops // 64, bytes_accessed=rows * pairs * PAIR, transcendentals=0,
        ),
        name="attend",
    )(qkv, bias)


def attend_back_kernel(
    qkv_ref, bias_ref, out_ref, log_ref, grad_ref, result_ref, key_acc, value_acc
):
    rows = qkv_ref.shape[0]
    low = lax.broadcasted_iota(jnp.int32, (1, PAIR), 1) < DH
    keys = qkv_ref[:, PAIR : 2 * PAIR]
    values = qkv_ref[:, 2 * PAIR :]
    bias = bias_ref[...]
    zero = jnp.zeros((), BF16)
    picks = (low, jnp.logical_not(low))
    head_keys = [jnp.where(pick, keys, zero) for pick in picks]
    for tile in range(rows // ROWS):
        at = slice(tile * ROWS, (tile + 1) * ROWS)
        query = qkv_ref[at, :PAIR]
        grad = grad_ref[at, :]
        both = grad.astype(F32) * out_ref[at, :].astype(F32)
        query_grad = jnp.zeros((ROWS, PAIR), F32)
        key_grad = jnp.zeros((rows, PAIR), F32)
        value_grad = jnp.zeros((rows, PAIR), F32)
        for head in range(2):
            pick = picks[head]
            mine = jnp.where(pick, query, zero)
            mine_grad = jnp.where(pick, grad, zero)
            delta = jnp.sum(jnp.where(pick, both, 0.0), axis=1, keepdims=True)
            logs = log_ref[at, head * DH : head * DH + 1]
            prob = jnp.exp(product_back(mine, keys) + bias - logs)
            d_prob = product_back(mine_grad, values)
            d_scores = (prob * (d_prob - delta)).astype(BF16)
            query_grad = query_grad + product(d_scores, head_keys[head])
            key_grad = key_grad + row_product(d_scores, mine, F32)
            value_grad = value_grad + row_product(prob.astype(BF16), mine_grad, F32)
        query_grad = query_grad * DH**-0.5
        result_ref[at, :PAIR] = query_grad.astype(BF16)
        if tile == 0:
            key_acc[...] = key_grad
            value_acc[...] = value_grad
        else:
            key_acc[...] += key_grad
            value_acc[...] += value_grad
    result_ref[:, PAIR : 2 * PAIR] = key_acc[...].astype(BF16)
    result_ref[:, 2 * PAIR :] = value_acc[...].astype(BF16)


def attend_back(qkv, bias, out, logs, grad, pairs, begin, into=()):
    rows = qkv.shape[0]
    wide = pl.BlockSpec((rows, 3 * PAIR), lambda i: (0, i + begin))
    narrow = pl.BlockSpec((rows, PAIR), lambda i: (0, i + begin))

    def kernel(*refs):
        attend_back_kernel(*refs[:5], *refs[5 + len(into) :])

    return pl.pallas_call(
        kernel,
        grid=(pairs,),
        in_specs=[wide, pl.BlockSpec((1, rows), lambda i: (0, 0)), narrow, narrow, narrow]
        + [pl.BlockSpec(memory_space=pl.ANY)] * len(into),
        out_specs=wide,
        out_shape=jax.ShapeDtypeStruct(qkv.shape, BF16),
        scratch_shapes=[pltpu.VMEM((rows, PAIR), F32)] * 2,
        input_output_aliases={5: 0} if into else {},
        cost_estimate=cheap(rows * rows),
        name="attend_back",
    )(qkv, bias, out, logs, grad, *into)


def normed_of(hidden):
    centred = hidden - jnp.mean(hidden, axis=-1, keepdims=True)
    spread = jnp.mean(centred * centred, axis=-1, keepdims=True)
    scale = lax.rsqrt(spread + norm_eps)
    return centred * scale, scale


def norm_back(grad, gain, unit, scale):
    inner = grad * gain
    return scale * (
        inner
        - jnp.mean(inner, axis=-1, keepdims=True)
        - unit * jnp.mean(inner * unit, axis=-1, keepdims=True)
    )


def finish_kernel(
    part_ref, high_ref, query_ref, key_ref, value_ref, out_ref,
    features_ref, query_sum_ref, value_sum_ref, up_sum_ref, *, half,
):
    total = part_ref[...].astype(F32) + high_ref[...].astype(F32)
    width = query_ref.shape[1]
    for pair in range(width // PAIR):
        at = slice(pair * PAIR, (pair + 1) * PAIR)
        for place_of, ref in enumerate((query_ref, key_ref, value_ref)):
            start = (3 * pair + place_of) * PAIR
            ref[:, at] = total[:half, start : start + PAIR]
        start = 3 * pair * PAIR
        query_sum_ref[:, at] = total[half : half + 1, start : start + PAIR]
        start = start + 2 * PAIR
        value_sum_ref[:, at] = total[half : half + 1, start : start + PAIR]
    out_ref[...] = total[:half, 3 * width :].T
    wide = features_ref.shape[1]
    for row in range(3):
        for side in range(2):
            at = 2 * row + side
            features_ref[at : at + 1, :] = total[
                half + 1 + row : half + 2 + row, side * wide : (side + 1) * wide
            ]
    up_sum_ref[...] = total[half + 4 : half + 5]


def finish(part, high, half, width):
    columns = part.shape[1]
    return pl.pallas_call(
        functools.partial(finish_kernel, half=half),
        out_shape=[jax.ShapeDtypeStruct((half, width), F32)] * 3
        + [
            jax.ShapeDtypeStruct((columns - 3 * width, half), F32),
            jax.ShapeDtypeStruct((6, columns // 2), F32),
            jax.ShapeDtypeStruct((1, width), F32),
            jax.ShapeDtypeStruct((1, width), F32),
            jax.ShapeDtypeStruct((1, columns), F32),
        ],
        cost_estimate=cheap(part.size),
        name="finish",
    )(part, high)


def weave(parts):
    lead = parts[0].shape[0]
    parts = [part.reshape(lead, -1, PAIR) for part in parts]
    return jnp.stack(parts, axis=2).reshape(lead, -1)


def unweave(woven):
    lead = woven.shape[0]
    woven = woven.reshape(lead, -1, 3, PAIR)
    return [woven[:, :, part].reshape(lead, -1) for part in range(3)]


def per_device(
    layer_in,
    lengths,
    out_grad,
    query_weight,
    key_weight,
    value_weight,
    out_weight,
    up_weight,
    down_weight,
    query_bias,
    value_bias,
    out_bias,
    up_bias,
    down_bias,
    norm_gain,
    norm_bias,
    final_gain,
    final_bias,
):
    fsdp = lax.axis_index("fsdp")
    plane, core = fsdp // 2, fsdp % 2
    high, low = lax.axis_index("ctx"), lax.axis_index("tp")
    planes = lax.axis_size("fsdp") // 2
    half = query_weight.shape[0]
    rows = layer_in.shape[1]
    width = layer_in.shape[2]
    heads_width = query_weight.shape[1]
    hidden = up_weight.shape[1]
    key = (2 * plane + low).astype(jnp.int32)[None]
    qkv_width = 3 * heads_width
    inner_gather = Gather(
        jnp.concatenate([weave([query_weight, key_weight, value_weight]), out_weight.T], axis=1)
    )
    mine_in = lax.dynamic_index_in_dim(layer_in, low, 0, keepdims=False)
    own = to_turned(mine_in)
    length = lax.dynamic_index_in_dim(to_turned(lengths), low, 0, keepdims=False)
    inner_gather.near()
    outer_shard = jnp.concatenate([up_weight, down_weight.T], axis=1)
    outer_gather = Gather(after(outer_shard, inner_gather.first, inner_gather.second))
    inner_gather.far((((0, qkv_width), (qkv_width, heads_width)),))
    arrived = inner_gather.last()
    other = to_core(own)
    vectors = to_first(after(jnp.concatenate([query_bias, value_bias, up_bias]), own, *arrived))
    if planes == 4:
        outer_gather.near(inner_gather.over_x, inner_gather.over_y, other)
    else:
        outer_gather.near()
    mine_grad = lax.dynamic_index_in_dim(out_grad, low, 0, keepdims=False)
    own_grad = to_turned(after(mine_grad, own))
    qkv_weight, out_t = inner_gather.placed(key, 0)
    own = after(own, outer_gather.unit)

    out_b, down_b, gain1, bias1, gain2, bias2 = (
        out_bias, down_bias, norm_gain, norm_bias, final_gain, final_bias
    )
    query_b = vectors[:heads_width]
    value_b = vectors[heads_width : 2 * heads_width]
    up_b = vectors[2 * heads_width :]
    qkv_b = weave([query_b[None], jnp.zeros_like(query_b)[None], value_b[None]])
    scales = weave(
        [
            jnp.full((1, heads_width), DH**-0.5, F32),
            jnp.ones((1, heads_width), F32),
            jnp.ones((1, heads_width), F32),
        ]
    )
    places = lax.iota(jnp.int32, rows)
    own_places = core * rows + places
    other_places = (1 - core) * rows + places
    valid = jnp.concatenate([own_places, other_places]) < length
    bias = jnp.where(valid, 0.0, masked_score).astype(F32)[None, :]
    row_valid = (own_places < length).astype(F32)[:, None]

    x = jnp.concatenate([own, other], axis=0)
    qkv = ((product(x, qkv_weight) + qkv_b) * scales).astype(BF16)
    merged, logs = attend(qkv, bias)
    if planes == 4:
        merged = after(merged, own_grad)
    outer_gather.far((((0, hidden), (hidden, hidden)),))
    attn_other = to_core(product_back(merged[rows:], out_t, BF16))
    attn = product_back(merged[:rows], out_t)
    first = own.astype(F32) + attn + attn_other.astype(F32) + out_b
    unit1, scale1 = normed_of(first)
    normed = unit1 * gain1 + bias1
    normed_own = normed.astype(BF16)
    normed_other = to_core(normed_own)
    up, down_t = outer_gather.placed(key, 0)
    activated, slope = column_call(
        up_kernel, "up", (normed_own, normed_other), up, (up_b[None],),
        ((2 * rows, BF16), (2 * rows, BF16)), 256,
    )
    ffn_other = to_core(product_back(activated[rows:], down_t, BF16))
    ffn = product_back(activated[:rows], down_t)
    second = normed + ffn + ffn_other.astype(F32) + down_b
    unit2, scale2 = normed_of(second)
    result = (unit2 * gain2 + bias2).astype(BF16)
    result = to_turned(result)
    result_pair = to_low(result)

    cot = own_grad.astype(F32) * row_valid
    final_gain_grad = jnp.sum(cot * unit2, axis=0)
    final_bias_grad = jnp.sum(cot, axis=0)
    d_second = norm_back(cot, gain2, unit2, scale2)
    d_ffn_own = d_second.astype(BF16)
    down_bias_grad = jnp.sum(d_ffn_own.astype(F32), axis=0)
    d_ffn_other = to_core(d_ffn_own)
    down_scatter = Scatter([(d_ffn_own, d_ffn_other, activated)], half)
    d_ffn = jnp.concatenate([d_ffn_own, after(d_ffn_other, *down_scatter.blocks)], axis=0)
    d_upper = (product(d_ffn, down_t) * slope.astype(F32)).astype(BF16)
    up_bias_grad = jnp.sum(d_upper.astype(F32), axis=0)
    sent = down_scatter.near(d_upper)
    up_scatter = Scatter([(normed_own, normed_other, after(d_upper, *sent))], half)
    d_upper = after(d_upper, *up_scatter.blocks)
    back_other = to_core(product_back(d_upper[rows:], up, BF16))
    back = product_back(d_upper[:rows], up)
    d_normed = d_second + after(back, result, *down_scatter.arrivals()) + back_other.astype(F32)
    norm_gain_grad = jnp.sum(d_normed * unit1, axis=0)
    norm_bias_grad = jnp.sum(d_normed, axis=0)
    d_first = norm_back(d_normed, gain1, unit1, scale1)
    d_attn_own = d_first.astype(BF16)
    out_bias_grad = jnp.sum(d_attn_own.astype(F32), axis=0)
    d_attn_other = to_core(d_attn_own)
    features = jnp.stack(
        [
            out_bias_grad,
            down_bias_grad,
            norm_gain_grad,
            norm_bias_grad,
            final_gain_grad,
            final_bias_grad,
        ]
    )
    extra = None
    if planes == 4:
        features = (features + to_core(features)).reshape(3, -1)
        extra = jnp.concatenate([features, up_bias_grad[None]], axis=0)
        extra = jnp.pad(extra, ((1, TAIL - 5), (0, 0)))
    d_attn = jnp.concatenate([d_attn_own, d_attn_other], axis=0)
    d_merged = product(d_attn, out_t, BF16)
    down_pair = down_scatter.own()
    pairs = heads_width // PAIR
    part = pairs // 2
    back_args = (qkv, bias, merged, logs)
    d_merged = after(d_merged, *down_pair)
    d_qkv = attend_back(*back_args, d_merged, part, 0)
    sent = up_scatter.near(d_qkv)
    down_part = down_scatter.part(d_qkv)
    down_high = to_high(down_part)
    d_merged = after(d_merged, d_qkv, result_pair, down_part, *sent)
    d_qkv = attend_back(*back_args, d_merged, pairs - part, part, (d_qkv,))
    inner_scatter = Scatter(
        [(own, other, d_qkv), (d_attn_own, d_attn_other, merged)], half, TAIL, extra
    )
    pair = up_scatter.own(*inner_scatter.blocks)
    d_qkv = after(d_qkv, *pair)
    d_back = after(d_qkv, down_high, *inner_scatter.blocks)
    back_other = to_core(product_back(d_back[rows:], qkv_weight, BF16))
    back = product_back(d_back[:rows], qkv_weight)
    total = d_first + back + back_other.astype(F32)
    total = total.astype(BF16)
    up_part = up_scatter.part(back)
    up_high = to_high(up_part)
    inner_scatter.near(total, up_part)
    total = to_turned(total)
    pair = inner_scatter.own()
    inner_part = inner_scatter.part()
    total_pair = to_low(after(total, inner_part))
    result_pair = after(result_pair, *pair)
    layer_out = jnp.where(
        low == 0, jnp.stack([result, result_pair]), jnp.stack([result_pair, result])
    )
    input_grad = jnp.where(
        low == 0, jnp.stack([total, total_pair]), jnp.stack([total_pair, total])
    ).astype(F32)
    inner_high = to_high(inner_part)

    down_grad = summed(down_part, down_high).T
    up_sums = summed(up_part, up_high)
    up_grad = up_sums[:half]
    inner_high = after(inner_high, total_pair)
    if planes == 4:
        query_grad, key_grad, value_grad, out_weight_grad, *sums = finish(
            inner_part, inner_high, half, heads_width
        )
        features = sums[0]
        query_bias_grad, value_bias_grad, up_bias_grad = (row[0] for row in sums[1:])
    else:
        inner_sums = summed(inner_part, inner_high)
        query_grad, key_grad, value_grad = unweave(inner_sums[:half, :qkv_width])
        out_weight_grad = inner_sums[:half, qkv_width:].T

        def spread(vector):
            empty = jnp.zeros_like(vector)
            return jnp.where(
                core == 0, jnp.concatenate([vector, empty]), jnp.concatenate([empty, vector])
            )

        sums = jnp.sum(d_qkv.astype(F32), axis=0, keepdims=True)
        query_sum, _, value_sum = (row[0] for row in unweave(sums))
        up_sum = up_bias_grad
        small = jnp.concatenate(
            [features.reshape(-1), spread(query_sum), spread(value_sum), spread(up_sum)]
        )
        small = lax.psum(small, AXES)
        features = small[: 6 * width].reshape(6, width)
        at = 6 * width

        def mine(start, size):
            return lax.dynamic_slice(small, (start + low * size,), (size,))

        query_bias_grad = mine(at, heads_width)
        value_bias_grad = mine(at + 2 * heads_width, heads_width)
        up_bias_grad = mine(at + 4 * heads_width, hidden)
    return (
        layer_out,
        input_grad,
        query_grad,
        key_grad,
        value_grad,
        out_weight_grad,
        up_grad,
        down_grad,
        query_bias_grad,
        value_bias_grad,
        features[0],
        up_bias_grad,
        features[1],
        features[2],
        features[3],
        features[4],
        features[5],
    )


def solution(mesh):
    in_specs = (
        P("fsdp", "ctx", None),
        P("fsdp"),
        P("fsdp", "ctx", None),
        P("fsdp", "tp"),
        P("fsdp", "tp"),
        P("fsdp", "tp"),
        P("tp", "fsdp"),
        P("fsdp", "tp"),
        P("tp", "fsdp"),
        P("tp"),
        P("tp"),
        P(),
        P("tp"),
        P(),
        P(),
        P(),
        P(),
        P(),
    )
    out_specs = (
        P("fsdp", "ctx", None),
        P("fsdp", "ctx", None),
        P("fsdp", "tp"),
        P("fsdp", "tp"),
        P("fsdp", "tp"),
        P("tp", "fsdp"),
        P("fsdp", "tp"),
        P("tp", "fsdp"),
        P("tp"),
        P("tp"),
        P(),
        P("tp"),
        P(),
        P(),
        P(),
        P(),
        P(),
    )
    return jax.shard_map(
        per_device, mesh=mesh, in_specs=in_specs, out_specs=out_specs, check_vma=False
    )
```
